32 devices in a mesh: tower: 4 (over y, x), rank: 8 (over z, core).
Axes of the slice: x: 2, y: 2, z: 4, core: 2. Of those that a mesh axis runs over, the one named last changes fastest.
Arguments:
- pooled: bfloat16 [2, 2048, 1024], P(None, ('tower', 'rank')), may hold values from -8 to 8
- feature_order: int32 [4, 4], P('tower'), may hold values from 0 to 3, as said below
- cross_weight: bfloat16 [4, 3, 512, 512], P('tower'), may hold values from -0.25 to 0.25
- cross_bias: float32 [4, 3, 512], P('tower'), may hold values from -3 to 3
- compress_weight: bfloat16 [4, 128, 512], P('tower'), may hold values from -0.25 to 0.25
- norm_gain: float32 [4, 128], P('tower'), may hold values from 0.1 to 1.9
- mlp_weight: bfloat16 [4096, 512], P(('tower', 'rank')), may hold values from -0.25 to 0.25
- mlp_bias: bfloat16 [4096], P(('tower', 'rank')), may hold values from -3 to 3
- out_weight: bfloat16 [4096], P(('tower', 'rank')), may hold values from -0.09375 to 0.09375
Outputs:
- logits: float32 [2, 8, 128], P(None, 'rank', 'tower')
The draws below stay inside these ranges and needn't reach their ends.
Inputs may be any that keep to these rules, and one draw needn't show every extreme that they name: `feature_order`: each row is an ordering of 0 to 3.
All inputs are finite; a program needn't handle non-finite values.
Results may differ from the reference program's by a relative error of at most 0.0076.
Values may be sent and summed in bfloat16 or wider, within the bound.
A program may use at most 64 MiB of HBM per device.

```python
import math
import jax
import jax.numpy as jnp
from jax import lax

E = 128
FT = 4
CD = 128
HID = 4096
LAYERS = 3
MB = 2
SAMP_DEV = 32
TD = 512
F = 16
ID = 512
SAMPLES = 1024
N_TOWER = 4
N_RANK = 8


def draw_pooled(key, part):
    first_key, second_key = jax.random.split(jax.random.fold_in(key, 11))
    shape = (MB, F * E, SAMPLES)
    base = jnp.clip(jax.random.normal(first_key, shape, jnp.float32), -4.0, 4.0)
    scales = jnp.exp(jax.random.uniform(second_key, (MB, 1, SAMPLES), jnp.float32, math.log(0.5), math.log(2.0)))
    return (base * scales).astype(jnp.bfloat16)


def draw_feature_order(key, part):
    keys = jax.random.split(jax.random.fold_in(key, 23), N_TOWER)
    return jax.vmap(lambda single: jax.random.permutation(single, FT))(keys).astype(jnp.int32)


def block_levels(key, shape, cuts, smallest, largest):
    loudness = 1.0
    for dim, blocks in cuts:
        steps = jax.random.uniform(jax.random.fold_in(jax.random.fold_in(key, 6), dim), (blocks,), jnp.float32, smallest / len(cuts), largest / len(cuts))
        loudness = loudness * jnp.repeat(jnp.exp(steps), shape[dim] // blocks).reshape((-1,) + (1,) * (len(shape) - 1 - dim))
    return loudness


def scatter_about(own_key, shape, width, bound, cuts=(), dtype=jnp.bfloat16):
    entries = width * jax.random.normal(own_key, shape, jnp.float32)
    if cuts:
        entries = entries * block_levels(own_key, shape, cuts, -0.22, 0.18)
    return jnp.clip(entries, -bound, bound).astype(dtype)


def setup_inputs(seed: int = 0) -> dict:
    key_list = jax.random.split(jax.random.key(seed), 10)
    return {
        "pooled": draw_pooled(jax.random.fold_in(key_list[9], 71), 0),
        "feature_order": draw_feature_order(jax.random.fold_in(key_list[9], 71), 0),
        "cross_weight": scatter_about(key_list[2], (N_TOWER, LAYERS, TD, TD), TD ** -0.5, 0.25, ((0, 4),)),
        "cross_bias": scatter_about(key_list[3], (N_TOWER, LAYERS, TD), 0.5, 3.0, ((0, 4),), jnp.float32),
        "compress_weight": scatter_about(key_list[4], (N_TOWER, CD, TD), TD ** -0.5, 0.25, ((0, 4),)),
        "norm_gain": jnp.clip(1.0 + 0.18 * jax.random.normal(key_list[5], (N_TOWER, CD), jnp.float32), 0.1, 1.9),
        "mlp_weight": scatter_about(key_list[6], (HID, ID), ID ** -0.5, 0.25, ((0, 32),)),
        "mlp_bias": scatter_about(key_list[7], (HID,), 0.5, 3.0, ((0, 32),)),
        "out_weight": scatter_about(key_list[8], (HID,), HID ** -0.5, 0.09375, ((0, 32),)),
    }


epsilon = 1e-06

def tower_block(first, weights, biases, compress, gain):
    first_f = first.astype(jnp.float32)
    current = first
    for layer in range(LAYERS):
        product = jnp.dot(weights[layer], current, preferred_element_type=jnp.float32) + biases[layer][:, None]
        current = (first_f * product + current.astype(jnp.float32)).astype(jnp.bfloat16)
    squeezed = jnp.dot(compress, current, preferred_element_type=jnp.float32)
    inverse_rms = lax.rsqrt(lax.optimization_barrier(jnp.mean(squeezed * squeezed, axis=0, keepdims=True)) + epsilon)
    return (squeezed * inverse_rms * gain[:, None]).astype(jnp.bfloat16)

def interact(joined):
    samples_now = joined.shape[1]
    values_f = joined.astype(jnp.float32).reshape(-1, CD, samples_now)
    gram = jnp.einsum('tck,uck->tuk', values_f, values_f, precision=lax.Precision.HIGHEST) / CD
    mixed = values_f + jnp.einsum('tuk,uck->tck', gram, values_f, precision=lax.Precision.HIGHEST)
    return mixed.reshape(-1, samples_now).astype(jnp.bfloat16)

def reference(pooled, feature_order, cross_weight, cross_bias, compress_weight, norm_gain, mlp_weight, mlp_bias, out_weight):
    results = []
    block_size = SAMP_DEV * N_TOWER
    for batch in range(MB):
        arrived = pooled[batch].reshape(N_TOWER, FT, E, SAMPLES)

        def one_tower(packed):
            blocks, slots, weights, biases, compress, gain = packed
            first = jnp.take(blocks, slots, axis=0).reshape(TD, SAMPLES)
            return tower_block(first, weights, biases, compress, gain)
        outputs = lax.map(one_tower, (arrived, feature_order, cross_weight, cross_bias, compress_weight, norm_gain))
        mixed = interact(outputs.reshape(ID, SAMPLES))
        pieces = mixed.reshape(ID, N_RANK, block_size).transpose(1, 0, 2)

        def one_block(piece):
            hidden = jnp.dot(mlp_weight, piece, preferred_element_type=jnp.float32) + mlp_bias.astype(jnp.float32)[:, None]
            return lax.optimization_barrier(jnp.sum(jax.nn.relu(hidden) * out_weight.astype(jnp.float32)[:, None], axis=0))
        results.append(lax.map(one_block, pieces))
    return jnp.stack(results)
```

```python
import functools

import jax
import jax.numpy as jnp
from jax import lax
from jax.experimental import pallas as pl
from jax.experimental.pallas import tpu as pltpu
from jax.sharding import PartitionSpec as P

E = 128
CD = 128
CORES = 2

epsilon = 1e-06
MESH = pl.DeviceIdType.MESH


def drain(ref, sem):
    pltpu.make_async_copy(ref, ref, sem).wait()


def fused(
    n_tower,
    n_rank,
    order_any,
    pooled,
    cross_w,
    cross_b,
    compress,
    gain,
    mlp_w,
    hid_b,
    hid_o,
    out,
    order,
    arrived,
    weights,
    compress_v,
    bias_v,
    flat_v,
    gain_v,
    bias_c,
    gain_c,
    first,
    state_a,
    state_b,
    towers,
    mixed,
    rows,
    packs_b,
    packs_o,
    flat_b,
    flat_o,
    hid_c,
    parts,
    load_sem,
    a2a_send,
    a2a_recv,
    row_send,
    row_recv,
    mate_recv,
    pack_send,
    pack_recv,
    tower_send,
    tower_recv,
    part_send,
    part_recv,
):
    micro = pooled.shape[0]
    block = arrived[0].shape[-1]
    layers, td = cross_w.shape[1], cross_w.shape[2]
    smalls = ((hid_b, packs_b), (hid_o, packs_o))
    chips = n_rank // CORES
    t = lax.axis_index("tower")
    r = lax.axis_index("rank")
    z = r // CORES
    c = lax.rem(r, CORES)
    mate = z * CORES + (1 - c)

    loads = [
        pltpu.make_async_copy(cross_b, bias_v, load_sem.at[0]),
        pltpu.make_async_copy(gain, gain_v, load_sem.at[0]),
        pltpu.make_async_copy(hid_b, packs_b.at[r], load_sem.at[0]),
        pltpu.make_async_copy(hid_o, packs_o.at[r], load_sem.at[0]),
        pltpu.make_async_copy(compress.at[0], compress_v, load_sem.at[0]),
        pltpu.make_async_copy(mlp_w, rows.at[r], load_sem.at[0]),
        pltpu.make_async_copy(order_any, order, load_sem.at[0]),
    ]
    own_loads = []
    for b in range(micro):
        own = pooled.at[b, :, pl.ds(pl.multiple_of(r * block, block), block)]
        own_loads.append(pltpu.make_async_copy(own, arrived[b].at[r], a2a_recv.at[b]))
    w_loads = [pltpu.make_async_copy(cross_w.at[0, l], weights.at[l], load_sem.at[1 + l]) for l in range(layers)]

    barrier = pltpu.get_barrier_semaphore()
    for d in range(1, n_rank):
        pl.semaphore_signal(barrier, inc=1, device_id={"rank": lax.rem(r + d, n_rank)}, device_id_type=MESH)
    for d in range(1, n_tower):
        pl.semaphore_signal(barrier, inc=1, device_id={"tower": lax.rem(t + d, n_tower)}, device_id_type=MESH)
    for copy in own_loads + loads + w_loads:
        copy.start()
    pl.semaphore_wait(barrier, n_rank + n_tower - 2)

    def spread(b, source, target, src_ref):
        return pltpu.make_async_remote_copy(
            src_ref=src_ref,
            dst_ref=arrived[b].at[source],
            send_sem=a2a_send.at[b],
            recv_sem=a2a_recv.at[b],
            device_id={"rank": target},
            device_id_type=MESH,
        )

    def chip_at(k):
        return lax.rem(z + k + chips, chips)

    others = [
        chip_at(k) * CORES + (c if twin == 0 else 1 - c)
        for k in sorted(range(chips), key=lambda k: -min(k, chips - k))
        for twin in range(CORES)
        if (k, twin) != (0, 0)
    ]
    for b in range(micro):
        for peer in others:
            columns = pl.ds(pl.multiple_of(peer * block, block), block)
            copy = spread(b, r, peer, pooled.at[b, :, columns])
            copy.start()

    half = rows.shape[1] // 2
    seen = set()

    def piece(k, h):
        return rows.at[chip_at(k) * CORES + c, pl.ds(h * half, half)]

    def row_copy(k, h, way, src_ref):
        return pltpu.make_async_remote_copy(
            src_ref=src_ref,
            dst_ref=piece(k, h),
            send_sem=row_send.at[0],
            recv_sem=row_recv.at[chip_at(k), h],
            device_id={"rank": chip_at(way) * CORES + c},
            device_id_type=MESH,
        )

    def arrive(k, h):
        if k % chips and (k % chips, h) not in seen:
            seen.add((k % chips, h))
            row_copy(k, h, 1, piece(k, h)).wait_recv()

    row_sends = []

    def hop(s):
        for h, way in ((0, 1), (1, -1), (1, 1), (0, -1)):
            reach = chips // 2 if (h, way) in ((0, 1), (1, -1)) else (chips - 1) // 2
            if s < reach:
                k = -way * s
                if s:
                    arrive(k, h)
                copy = row_copy(k, h, way, piece(k, h) if s else mlp_w.at[pl.ds(h * half, half)])
                copy.start()
                row_sends.append(copy)

    def mate_copy(k, src_ref):
        return pltpu.make_async_remote_copy(
            src_ref=src_ref,
            dst_ref=rows.at[chip_at(k) * CORES + c],
            send_sem=row_send.at[0],
            recv_sem=mate_recv.at[k],
            device_id={"rank": mate},
            device_id_type=MESH,
        )

    def share(k):
        for h in range(2):
            arrive(k, h)
        copy = mate_copy(k, rows.at[chip_at(k) * CORES + c] if k else mlp_w)
        copy.start()
        row_sends.append(copy)

    for d in range(1, n_rank):
        for i, (source, target) in enumerate(smalls):
            copy = pltpu.make_async_remote_copy(
                src_ref=source,
                dst_ref=target.at[r],
                send_sem=pack_send.at[i],
                recv_sem=pack_recv.at[i],
                device_id={"rank": lax.rem(r + d, n_rank)},
                device_id_type=MESH,
            )
            copy.start()

    hop(0)
    share(0)
    near = [k for k in range(1, chips) if min(k, chips - k) == 1]
    far = [k for k in sorted(range(1, chips), key=lambda k: min(k, chips - k)) if k not in near]

    for copy in loads:
        copy.wait()
    for l in range(layers):
        flat_v[l : l + 1, :] = bias_v[l]
    bias_c[...] = flat_v[...].T
    gain_c[...] = jnp.broadcast_to(gain_v[...], (8, CD)).T

    per_feature = n_rank // order.shape[1]
    height = arrived[0].shape[1]
    for b in range(micro):
        cols = slice(b * block, (b + 1) * block)
        drain(arrived[b], a2a_recv.at[b])
        for slot in range(order.shape[1]):
            feature = order[0, slot]
            for h in range(per_feature):
                first[slot * E + h * height : slot * E + (h + 1) * height, cols] = arrived[b][
                    feature * per_feature + h
                ]

        current, spare = first, state_a
        for l in range(layers):
            if b == 0:
                w_loads[l].wait()
            for m in range(0, td, E):
                here = slice(m, m + E)
                product = (
                    jnp.dot(weights[l, here, :], current[:, cols], preferred_element_type=jnp.float32)
                    + bias_c[here, l : l + 1]
                )
                spare[here, cols] = (
                    first[here, cols].astype(jnp.float32) * product
                    + current[here, cols].astype(jnp.float32)
                ).astype(jnp.bfloat16)
            current, spare = spare, (state_b if spare is state_a else state_a)
        squeezed = jnp.dot(compress_v[...], current[:, cols], preferred_element_type=jnp.float32)
        inverse_rms = lax.rsqrt(jnp.mean(squeezed * squeezed, axis=0, keepdims=True) + epsilon)
        towers[b][t] = (squeezed * inverse_rms * gain_c[:, 0:1]).astype(jnp.bfloat16)

        for d in range(1, n_tower):
            copy = pltpu.make_async_remote_copy(
                src_ref=towers[b].at[t],
                dst_ref=towers[b].at[t],
                send_sem=tower_send.at[b],
                recv_sem=tower_recv.at[b],
                device_id={"tower": lax.rem(t + d, n_tower)},
                device_id_type=MESH,
            )
            copy.start()

    hop(1)
    for k in near:
        share(k)
    for step in range(2, chips // 2):
        hop(step)
    for i, (source, target) in enumerate(smalls):
        drain(target.at[: n_rank - 1], pack_recv.at[i])
    for s in range(n_rank):
        flat_b[s : s + 1, :] = packs_b[s].astype(jnp.float32)
        flat_o[s : s + 1, :] = packs_o[s].astype(jnp.float32)
    turned_b = flat_b[...].T
    turned_o = flat_o[...].T
    for s in range(n_rank):
        hid_c[s, 0] = turned_b[:, s : s + 1]
        hid_c[s, 1] = turned_o[:, s : s + 1]

    for b in range(micro):
        cols = slice(b * block, (b + 1) * block)
        drain(towers[b].at[: n_tower - 1], tower_recv.at[b])
        values = [towers[b][u].astype(jnp.float32) for u in range(n_tower)]
        gram = {}
        for u in range(n_tower):
            for v in range(u, n_tower):
                gram[u, v] = gram[v, u] = jnp.sum(values[u] * values[v], axis=0, keepdims=True) / CD
        for u in range(n_tower):
            total = values[u]
            for v in range(n_tower):
                total = total + gram[u, v] * values[v]
            mixed[u * CD : (u + 1) * CD, cols] = total.astype(jnp.bfloat16)

    score = jnp.zeros((rows.shape[1], mixed.shape[1]), jnp.float32)

    def add(s, score):
        hidden = jnp.dot(rows[s], mixed[...], preferred_element_type=jnp.float32) + hid_c[s, 0]
        return score + jnp.maximum(hidden, 0.0) * hid_c[s, 1]

    def add_mate(k, score):
        s = chip_at(k) * CORES + 1 - c
        pltpu.make_async_remote_copy(
            src_ref=rows.at[s],
            dst_ref=rows.at[s],
            send_sem=row_send.at[0],
            recv_sem=mate_recv.at[k],
            device_id={"rank": mate},
            device_id_type=MESH,
        ).wait_recv()
        return add(s, score)

    for k in [0] + near:
        score = add(chip_at(k) * CORES + c, score)
    for k in [0] + near:
        score = add_mate(k, score)
    for k in far:
        share(k)
        score = add(chip_at(k) * CORES + c, score)
    for k in far:
        score = add_mate(k, score)
    parts[t] = jnp.sum(score, axis=0, keepdims=True)

    for d in range(1, n_tower):
        copy = pltpu.make_async_remote_copy(
            src_ref=parts.at[t],
            dst_ref=parts.at[t],
            send_sem=part_send.at[0],
            recv_sem=part_recv.at[0],
            device_id={"tower": lax.rem(t + d, n_tower)},
            device_id_type=MESH,
        )
        copy.start()

    for b in range(micro):
        drain(arrived[b].at[: n_rank - 1], a2a_send.at[b])
        drain(towers[b].at[: n_tower - 1], tower_send.at[b])
    for i, (source, target) in enumerate(smalls):
        drain(target.at[: n_rank - 1], pack_send.at[i])
    for copy in row_sends:
        copy.wait_send()
    drain(parts.at[: n_tower - 1], part_recv.at[0])
    logits = parts[0]
    for u in range(1, n_tower):
        logits = logits + parts[u]
    width = block // n_tower
    for u in range(n_tower):

        @pl.when(t == u)
        def _():
            for b in range(micro):
                out[b] = logits[:, b * block + u * width : b * block + (u + 1) * width]

    drain(parts.at[: n_tower - 1], part_send.at[0])


def in_one_kernel(
    n_tower, n_rank, pooled, order, cross_w, cross_b, compress, gain, mlp_w, mlp_bias, out_weight
):
    micro, height, samples = pooled.shape
    block = samples // n_rank
    _, layers, td, _ = cross_w.shape
    hid, width = mlp_w.shape
    chips = n_rank // CORES
    every = micro * block
    bf16, f32 = jnp.bfloat16, jnp.float32
    dma = pltpu.SemaphoreType.DMA
    hbm = pl.BlockSpec(memory_space=pl.ANY)
    return pl.pallas_call(
        functools.partial(fused, n_tower, n_rank),
        out_shape=pltpu.VMEM((micro, 1, block // n_tower), f32),
        in_specs=[hbm] * 9,
        out_specs=pl.BlockSpec(memory_space=pltpu.VMEM),
        scratch_shapes=[
            pltpu.SMEM(order.shape, order.dtype),
            [pltpu.VMEM((n_rank, height, block), bf16)] * micro,
            pltpu.VMEM((layers, td, td), bf16),
            pltpu.VMEM((CD, td), bf16),
            pltpu.VMEM((layers, 1, td), f32),
            pltpu.VMEM((8, td), f32),
            pltpu.VMEM((1, CD), f32),
            pltpu.VMEM((td, 8), f32),
            pltpu.VMEM((CD, 8), f32),
            pltpu.VMEM((td, every), bf16),
            pltpu.VMEM((td, every), bf16),
            pltpu.VMEM((td, every), bf16),
            [pltpu.VMEM((n_tower, CD, block), bf16)] * micro,
            pltpu.VMEM((width, every), bf16),
            pltpu.VMEM((n_rank, hid, width), bf16),
            pltpu.VMEM((n_rank, 1, hid), bf16),
            pltpu.VMEM((n_rank, 1, hid), bf16),
            pltpu.VMEM((n_rank, hid), f32),
            pltpu.VMEM((n_rank, hid), f32),
            pltpu.VMEM((n_rank, 2, hid, 1), f32),
            pltpu.VMEM((n_tower, 1, every), f32),
            dma((1 + layers,)),
            dma((micro,)),
            dma((micro,)),
            dma((1,)),
            dma((chips, 2)),
            dma((chips,)),
            dma((2,)),
            dma((2,)),
            dma((micro,)),
            dma((micro,)),
            dma((1,)),
            dma((1,)),
        ],
        compiler_params=pltpu.CompilerParams(collective_id=0, has_side_effects=True),
    )(
        order,
        pooled,
        cross_w,
        cross_b.swapaxes(0, 1),
        compress,
        gain,
        mlp_w,
        mlp_bias[None],
        out_weight[None],
    )


def tower_block(first, weights, biases, compress, gain):
    first_f = first.astype(jnp.float32)
    current = first
    for layer in range(weights.shape[0]):
        product = (
            jnp.dot(weights[layer], current, preferred_element_type=jnp.float32)
            + biases[layer][:, None]
        )
        current = (first_f * product + current.astype(jnp.float32)).astype(jnp.bfloat16)
    squeezed = jnp.dot(compress, current, preferred_element_type=jnp.float32)
    inverse_rms = lax.rsqrt(jnp.mean(squeezed * squeezed, axis=0, keepdims=True) + epsilon)
    return (squeezed * inverse_rms * gain[:, None]).astype(jnp.bfloat16)


def interact(joined):
    samples_now = joined.shape[1]
    values_f = joined.astype(jnp.float32).reshape(-1, CD, samples_now)
    gram = jnp.einsum("tck,uck->tuk", values_f, values_f, precision=lax.Precision.HIGHEST) / CD
    mixed = values_f + jnp.einsum("tuk,uck->tck", gram, values_f, precision=lax.Precision.HIGHEST)
    return mixed.reshape(-1, samples_now).astype(jnp.bfloat16)


def logit_terms(hidden_rows, hidden_bias, hidden_out, features):
    hidden = (
        jnp.dot(hidden_rows, features, preferred_element_type=jnp.float32)
        + hidden_bias.astype(jnp.float32)[:, None]
    )
    return jnp.sum(
        jax.nn.relu(hidden) * hidden_out.astype(jnp.float32)[:, None], axis=0, keepdims=True
    )


def by_collectives(
    pooled,
    feature_order,
    cross_weight,
    cross_bias,
    compress_weight,
    norm_gain,
    mlp_weight,
    mlp_bias,
    out_weight,
):
    micro_count = pooled.shape[0]
    arriving = [
        lax.all_to_all(pooled[batch], "rank", split_axis=1, concat_axis=0, tiled=True)
        for batch in range(micro_count)
    ]
    hidden_rows, hidden_bias, hidden_out = (
        lax.all_gather(mlp_weight, "rank", axis=0, tiled=True),
        lax.all_gather(mlp_bias, "rank", axis=0, tiled=True),
        lax.all_gather(out_weight, "rank", axis=0, tiled=True),
    )
    results = []
    for batch in range(micro_count):
        arrived = arriving[batch]
        samples_here = arrived.shape[1]
        first = jnp.take(arrived.reshape(-1, E, samples_here), feature_order[0], axis=0).reshape(
            -1, samples_here
        )
        compressed = tower_block(
            first, cross_weight[0], cross_bias[0], compress_weight[0], norm_gain[0]
        )
        all_towers = lax.all_gather(compressed, "tower", axis=0, tiled=True)
        partial_value = logit_terms(hidden_rows, hidden_bias, hidden_out, interact(all_towers))
        logit_row = lax.psum_scatter(partial_value, "tower", scatter_dimension=1, tiled=True)
        results.append(logit_row)
    return jnp.stack(results)


def fits(mesh, pooled, mlp_w):
    height, hid = pooled.shape[1], mlp_w.shape[0]
    return mesh.shape["rank"] % CORES == 0 and E % height == 0 and height % 16 == 0 and hid % 128 == 0


def solution(mesh):
    def on_device(*args):
        if fits(mesh, args[0], args[6]):
            return in_one_kernel(mesh.shape["tower"], mesh.shape["rank"], *args)
        return by_collectives(*args)

    return jax.shard_map(
        on_device,
        mesh=mesh,
        in_specs=(
            P(None, ("tower", "rank"), None),
            P("tower", None),
            P("tower", None, None, None),
            P("tower", None, None),
            P("tower", None, None),
            P("tower", None),
            P(("tower", "rank"), None),
            P(("tower", "rank")),
            P(("tower", "rank")),
        ),
        out_specs=P(None, "rank", "tower"),
        check_vma=False,
    )
```

```python
import functools

import jax
import jax.numpy as jnp
from jax import lax
from jax.experimental import pallas as pl
from jax.experimental.pallas import tpu as pltpu
from jax.sharding import PartitionSpec as P

E = 128
CD = 128
CORES = 2
LINE = 4
PIECES = 2

epsilon = 1e-06
MESH = pl.DeviceIdType.MESH


def drain(ref, sem):
    pltpu.make_async_copy(ref, ref, sem).wait()


def fused(
    n_tower,
    n_rank,
    order_any,
    pooled,
    cross_w,
    cross_b,
    compress,
    gain,
    mlp_w,
    hid_b,
    hid_o,
    out,
    order,
    arrived,
    weights,
    compress_v,
    bias_v,
    flat_v,
    gain_v,
    bias_c,
    gain_c,
    first,
    state_a,
    state_b,
    towers,
    mixed,
    rows,
    packs,
    flat,
    hid_c,
    score,
    parts,
    aside,
    diagonal,
    load_sem,
    a2a_send,
    a2a_recv,
    row_send,
    row_recv,
    pack_send,
    pack_recv,
    tower_send,
    tower_recv,
    mix_send,
    mix_recv,
    part_send,
    part_recv,
):
    micro = pooled.shape[0]
    block = arrived[0].shape[-1]
    layers, td = cross_w.shape[1], cross_w.shape[2]
    hid = mlp_w.shape[0]
    piece = hid // PIECES
    chunks = [(b, j) for b in range(micro) for j in range(CORES)]
    t = lax.axis_index("tower")
    r = lax.axis_index("rank")
    z = r // CORES
    c = lax.rem(r, CORES)
    mate = z * CORES + (1 - c)
    half = z // 2
    here, there = 1 + half, 2 - half
    inner = z == here
    outer = z != here
    steps = [1 << i for i in range(n_tower.bit_length() - 1)]

    barrier = pltpu.get_barrier_semaphore()

    def greet(**device):
        pl.semaphore_signal(barrier, inc=1, device_id=device, device_id_type=MESH)

    own_loads = [
        pltpu.make_async_copy(
            pooled.at[b, :, pl.ds(pl.multiple_of(((2 * half + c) * CORES + j) * block, block), block)],
            arrived[q].at[r],
            a2a_recv.at[q],
        )
        for q, (b, j) in enumerate(chunks)
    ]
    own_packs = [pltpu.make_async_copy(ref, packs.at[z, i], pack_recv.at[0]) for i, ref in enumerate((hid_b, hid_o))]
    loads = [
        pltpu.make_async_copy(cross_b, bias_v, load_sem.at[0]),
        pltpu.make_async_copy(gain, gain_v, load_sem.at[0]),
        pltpu.make_async_copy(compress.at[0], compress_v, load_sem.at[0]),
        pltpu.make_async_copy(mlp_w, rows.at[z], load_sem.at[0]),
        pltpu.make_async_copy(order_any, order, load_sem.at[0]),
    ]
    w_loads = [pltpu.make_async_copy(cross_w.at[0, l], weights.at[l], load_sem.at[1 + l]) for l in range(layers)]

    def send_block(q, chip, core):
        b, j = chunks[q]
        rank = ((chip // 2) * 2 + core) * CORES + j
        pltpu.make_async_remote_copy(
            src_ref=pooled.at[b, :, pl.ds(pl.multiple_of(rank * block, block), block)],
            dst_ref=arrived[q].at[r],
            send_sem=a2a_send.at[0],
            recv_sem=a2a_recv.at[q],
            device_id={"rank": chip * CORES + core},
            device_id_type=MESH,
        ).start()

    def send_rows(chip):
        for p in range(PIECES):
            pltpu.make_async_remote_copy(
                src_ref=mlp_w.at[pl.ds(p * piece, piece)],
                dst_ref=rows.at[z, pl.ds(p * piece, piece)],
                send_sem=row_send.at[0],
                recv_sem=row_recv.at[z, p],
                device_id={"rank": chip * CORES + c},
                device_id_type=MESH,
            ).start()

    def send_packs(chip):
        for i, ref in enumerate((hid_b, hid_o)):
            pltpu.make_async_remote_copy(
                src_ref=ref,
                dst_ref=packs.at[z, i],
                send_sem=pack_send.at[0],
                recv_sem=pack_recv.at[0],
                device_id={"rank": chip * CORES + c},
                device_id_type=MESH,
            ).start()

    @pl.when(outer)
    def _():
        pl.semaphore_wait(barrier, 2 * CORES)
        for q in range(len(chunks)):
            for chip in (there, here):
                for core in (c, 1 - c):
                    send_block(q, chip, core)
        for chip in (there, here):
            send_packs(chip)
        for chip in (there, here):
            send_rows(chip)

    width = block // n_tower

    def finish(count):
        drain(parts.at[:count], part_recv.at[0])
        logits = parts[0]
        for u in range(1, n_tower * CORES):
            logits = logits + parts[u]
        for u in range(n_tower):

            @pl.when(t == u)
            def _():
                for b in range(micro):
                    out[b] = logits[:, b * block + u * width : b * block + (u + 1) * width]

    @pl.when(inner)
    def _():
        for k in range(CORES):
            greet(rank=there * CORES + k)
        for k in range(CORES):
            greet(rank=3 * half * CORES + k)
            greet(rank=3 * (1 - half) * CORES + k)
        greet(rank=mate)
        for d in steps:
            greet(tower=t ^ d)
        for copy in own_loads + own_packs + loads + w_loads:
            copy.start()
        pl.semaphore_wait(barrier, 2 * CORES - 1 + len(steps))
        if len(steps) > 1:
            pl.semaphore_signal(diagonal, inc=1, device_id={"tower": t ^ 1}, device_id_type=MESH)
        for q in range(len(chunks)):
            for core in (c, 1 - c):
                send_block(q, there, core)
            send_block(q, here, 1 - c)
        send_packs(there)
        send_rows(there)

        for copy in loads:
            copy.wait()
        for l in range(layers):
            flat_v[l : l + 1, :] = bias_v[l]
        bias_c[...] = flat_v[...].T
        gain_c[...] = jnp.broadcast_to(gain_v[...], (8, CD)).T
        for q in range(len(chunks)):
            score[q] = jnp.zeros(score.shape[1:], jnp.float32)

        per_feature = n_rank // order.shape[1]
        height = arrived[0].shape[1]

        def tower(q):
            cols = slice(q * block, (q + 1) * block)
            drain(arrived[q], a2a_recv.at[q])
            for slot in range(order.shape[1]):
                feature = order[0, slot]
                for h in range(per_feature):
                    first[slot * E + h * height : slot * E + (h + 1) * height, cols] = arrived[q][
                        feature * per_feature + h
                    ]

            current, spare = first, state_a
            for l in range(layers):
                if q == 0:
                    w_loads[l].wait()
                for m in range(0, td, E):
                    at = slice(m, m + E)
                    product = (
                        jnp.dot(weights[l, at, :], current[:, cols], preferred_element_type=jnp.float32)
                        + bias_c[at, l : l + 1]
                    )
                    spare[at, cols] = (
                        first[at, cols].astype(jnp.float32) * product
                        + current[at, cols].astype(jnp.float32)
                    ).astype(jnp.bfloat16)
                current, spare = spare, (state_b if spare is state_a else state_a)
            squeezed = jnp.dot(compress_v[...], current[:, cols], preferred_element_type=jnp.float32)
            inverse_rms = lax.rsqrt(jnp.mean(squeezed * squeezed, axis=0, keepdims=True) + epsilon)
            towers[q][t] = (squeezed * inverse_rms * gain_c[:, 0:1]).astype(jnp.bfloat16)
            if q == 0 and len(steps) > 1:
                pl.semaphore_wait(diagonal, 1)
            for d in range(n_tower - 1, 0, -1):
                pltpu.make_async_remote_copy(
                    src_ref=towers[q].at[t],
                    dst_ref=towers[q].at[t],
                    send_sem=tower_send.at[0],
                    recv_sem=tower_recv.at[q],
                    device_id={"tower": t ^ d},
                    device_id_type=MESH,
                ).start()

        def mix(q):
            drain(towers[q].at[: n_tower - 1], tower_recv.at[q])
            values = [towers[q][u].astype(jnp.float32) for u in range(n_tower)]
            gram = {}
            for u in range(n_tower):
                for v in range(u, n_tower):
                    gram[u, v] = gram[v, u] = jnp.sum(values[u] * values[v], axis=0, keepdims=True) / CD
            for u in range(n_tower):
                total = values[u]
                for v in range(n_tower):
                    total = total + gram[u, v] * values[v]
                mixed[q][u * CD : (u + 1) * CD, :block] = total.astype(jnp.bfloat16)
            pltpu.make_async_remote_copy(
                src_ref=mixed[q].at[:, pl.ds(0, block)],
                dst_ref=mixed[q].at[:, pl.ds(block, block)],
                send_sem=mix_send.at[0],
                recv_sem=mix_recv.at[q],
                device_id={"rank": mate},
                device_id_type=MESH,
            ).start()

        def mate_mixed(q):
            drain(mixed[q].at[:, pl.ds(block, block)], mix_recv.at[q])

        def landed(s, p):
            drain(rows.at[s, pl.ds(p * piece, piece)], row_recv.at[s, p])

        def add(q, s, lo=0, hi=hid):
            hidden = jnp.dot(rows[s, lo:hi, :], mixed[q][...], preferred_element_type=jnp.float32)
            bias, weight = hid_c[s, 0, lo:hi, :], hid_c[s, 1, lo:hi, :]
            for k in range(CORES):
                at = slice(k * block, (k + 1) * block)
                terms = jnp.maximum(hidden[:, at] + bias, 0.0) * weight
                score[q, :, at] = score[q, :, at] + jnp.sum(terms.reshape(-1, 8, block), axis=0)

        def prepare():
            drain(packs, pack_recv.at[0])
            for s in range(packs.shape[0]):
                for i in range(2):
                    flat[2 * s + i : 2 * s + i + 1, :] = packs[s, i].astype(jnp.float32)
            turned = flat[...].T
            for s in range(packs.shape[0]):
                for i in range(2):
                    hid_c[s, i] = jnp.broadcast_to(turned[:, 2 * s + i : 2 * s + i + 1], (hid, block))

        far, near = 3 * (1 - half), 3 * half
        count = len(chunks)
        for q in range(count):
            tower(q)
            if q >= 2:
                mix(q - 2)
            if q == count - 1:
                prepare()
        mate_mixed(0)
        add(0, here)
        mix(count - 2)
        mate_mixed(1)
        add(1, here)
        mix(count - 1)
        for p in range(PIECES):
            landed(there, p)
        for p in range(PIECES):
            landed(far, p)
        for s in (there, far):
            for q in range(2):
                add(q, s)
        for q in range(2, count):
            mate_mixed(q)
            for s in (here, there, far):
                add(q, s)
        for p in range(PIECES):
            landed(near, p)
            for q in range(count):
                add(q, near, p * piece, (p + 1) * piece)

        me = t * CORES + c
        for q, (b, j) in enumerate(chunks):
            at = slice(b * block, (b + 1) * block)
            aside[c, j, :, at] = jnp.sum(score[q, :, :block], axis=0, keepdims=True)
            aside[1 - c, j, :, at] = jnp.sum(score[q, :, block:], axis=0, keepdims=True)
        for d in range(n_tower - 1, -1, -1):
            for k in (half, 1 - half):
                for j in range(CORES):
                    rank = (2 * half + k) * CORES + j

                    def hand_over(k=k, j=j, rank=rank, d=d):
                        pltpu.make_async_remote_copy(
                            src_ref=aside.at[k, j],
                            dst_ref=parts.at[me],
                            send_sem=part_send.at[0],
                            recv_sem=part_recv.at[0],
                            device_id={"tower": t ^ d, "rank": rank},
                            device_id_type=MESH,
                        ).start()

                    if d:
                        hand_over()
                    else:
                        pl.when(rank != r)(hand_over)
        parts[me] = aside[1 - half, c]

        for q in range(count):
            drain(arrived[q].at[:CORES + 1], a2a_send.at[0])
            drain(towers[q].at[: n_tower - 1], tower_send.at[0])
            drain(mixed[q].at[:, pl.ds(0, block)], mix_send.at[0])
        drain(packs.at[0], pack_send.at[0])
        drain(rows.at[0], row_send.at[0])
        finish(n_tower * CORES - 1)
        drain(parts, part_send.at[0])
        drain(parts.at[: n_tower * CORES - 1], part_send.at[0])

    @pl.when(outer)
    def _():
        for q in range(len(chunks)):
            drain(arrived[q].at[: 2 * CORES], a2a_send.at[0])
        drain(packs.at[:2], pack_send.at[0])
        drain(rows.at[:2], row_send.at[0])
        finish(n_tower * CORES)


def in_one_kernel(
    n_tower, n_rank, pooled, order, cross_w, cross_b, compress, gain, mlp_w, mlp_bias, out_weight
):
    micro, height, samples = pooled.shape
    block = samples // n_rank
    _, layers, td, _ = cross_w.shape
    hid, width = mlp_w.shape
    chips = n_rank // CORES
    count = micro * CORES
    every = count * block
    bf16, f32 = jnp.bfloat16, jnp.float32
    dma = pltpu.SemaphoreType.DMA
    hbm = pl.BlockSpec(memory_space=pl.ANY)
    return pl.pallas_call(
        functools.partial(fused, n_tower, n_rank),
        out_shape=pltpu.VMEM((micro, 1, block // n_tower), f32),
        in_specs=[hbm] * 9,
        out_specs=pl.BlockSpec(memory_space=pltpu.VMEM),
        scratch_shapes=[
            pltpu.SMEM(order.shape, order.dtype),
            [pltpu.VMEM((n_rank, height, block), bf16)] * count,
            pltpu.VMEM((layers, td, td), bf16),
            pltpu.VMEM((CD, td), bf16),
            pltpu.VMEM((layers, 1, td), f32),
            pltpu.VMEM((8, td), f32),
            pltpu.VMEM((1, CD), f32),
            pltpu.VMEM((td, 8), f32),
            pltpu.VMEM((CD, 8), f32),
            pltpu.VMEM((td, every), bf16),
            pltpu.VMEM((td, every), bf16),
            pltpu.VMEM((td, every), bf16),
            [pltpu.VMEM((n_tower, CD, block), bf16)] * count,
            [pltpu.VMEM((width, CORES * block), bf16)] * count,
            pltpu.VMEM((chips, hid, width), bf16),
            pltpu.VMEM((chips, 2, 1, hid), bf16),
            pltpu.VMEM((2 * chips, hid), f32),
            pltpu.VMEM((chips, 2, hid, block), f32),
            pltpu.VMEM((count, 8, CORES * block), f32),
            pltpu.VMEM((n_tower * CORES, 1, micro * block), f32),
            pltpu.VMEM((CORES, CORES, 1, micro * block), f32),
            pltpu.SemaphoreType.REGULAR,
            dma((1 + layers,)),
            dma((1,)),
            dma((count,)),
            dma((1,)),
            dma((chips, PIECES)),
            dma((1,)),
            dma((1,)),
            dma((1,)),
            dma((count,)),
            dma((1,)),
            dma((count,)),
            dma((1,)),
            dma((1,)),
        ],
        compiler_params=pltpu.CompilerParams(collective_id=0, has_side_effects=True),
    )(
        order,
        pooled,
        cross_w,
        cross_b.swapaxes(0, 1),
        compress,
        gain,
        mlp_w,
        mlp_bias[None],
        out_weight[None],
    )


def tower_block(first, weights, biases, compress, gain):
    first_f = first.astype(jnp.float32)
    current = first
    for layer in range(weights.shape[0]):
        product = (
            jnp.dot(weights[layer], current, preferred_element_type=jnp.float32)
            + biases[layer][:, None]
        )
        current = (first_f * product + current.astype(jnp.float32)).astype(jnp.bfloat16)
    squeezed = jnp.dot(compress, current, preferred_element_type=jnp.float32)
    inverse_rms = lax.rsqrt(jnp.mean(squeezed * squeezed, axis=0, keepdims=True) + epsilon)
    return (squeezed * inverse_rms * gain[:, None]).astype(jnp.bfloat16)


def interact(joined):
    samples_now = joined.shape[1]
    values_f = joined.astype(jnp.float32).reshape(-1, CD, samples_now)
    gram = jnp.einsum("tck,uck->tuk", values_f, values_f, precision=lax.Precision.HIGHEST) / CD
    mixed = values_f + jnp.einsum("tuk,uck->tck", gram, values_f, precision=lax.Precision.HIGHEST)
    return mixed.reshape(-1, samples_now).astype(jnp.bfloat16)


def logit_terms(hidden_rows, hidden_bias, hidden_out, features):
    hidden = (
        jnp.dot(hidden_rows, features, preferred_element_type=jnp.float32)
        + hidden_bias.astype(jnp.float32)[:, None]
    )
    return jnp.sum(
        jax.nn.relu(hidden) * hidden_out.astype(jnp.float32)[:, None], axis=0, keepdims=True
    )


def by_collectives(
    pooled,
    feature_order,
    cross_weight,
    cross_bias,
    compress_weight,
    norm_gain,
    mlp_weight,
    mlp_bias,
    out_weight,
):
    micro_count = pooled.shape[0]
    arriving = [
        lax.all_to_all(pooled[batch], "rank", split_axis=1, concat_axis=0, tiled=True)
        for batch in range(micro_count)
    ]
    hidden_rows, hidden_bias, hidden_out = (
        lax.all_gather(mlp_weight, "rank", axis=0, tiled=True),
        lax.all_gather(mlp_bias, "rank", axis=0, tiled=True),
        lax.all_gather(out_weight, "rank", axis=0, tiled=True),
    )
    results = []
    for batch in range(micro_count):
        arrived = arriving[batch]
        samples_here = arrived.shape[1]
        first = jnp.take(arrived.reshape(-1, E, samples_here), feature_order[0], axis=0).reshape(
            -1, samples_here
        )
        compressed = tower_block(
            first, cross_weight[0], cross_bias[0], compress_weight[0], norm_gain[0]
        )
        all_towers = lax.all_gather(compressed, "tower", axis=0, tiled=True)
        partial_value = logit_terms(hidden_rows, hidden_bias, hidden_out, interact(all_towers))
        logit_row = lax.psum_scatter(partial_value, "tower", scatter_dimension=1, tiled=True)
        results.append(logit_row)
    return jnp.stack(results)


def fits(mesh, pooled, mlp_w):
    towers, ranks = mesh.shape["tower"], mesh.shape["rank"]
    height, hid = pooled.shape[1], mlp_w.shape[0]
    return (
        ranks == LINE * CORES
        and towers in (1, 2, 4)
        and E % height == 0
        and height % 16 == 0
        and hid % 128 == 0
        and (pooled.shape[2] // ranks) % 128 == 0
    )


def solution(mesh):
    def on_device(*args):
        if fits(mesh, args[0], args[6]):
            return in_one_kernel(mesh.shape["tower"], mesh.shape["rank"], *args)
        return by_collectives(*args)

    return jax.shard_map(
        on_device,
        mesh=mesh,
        in_specs=(
            P(None, ("tower", "rank"), None),
            P("tower", None),
            P("tower", None, None, None),
            P("tower", None, None),
            P("tower", None, None),
            P("tower", None),
            P(("tower", "rank"), None),
            P(("tower", "rank")),
            P(("tower", "rank")),
        ),
        out_specs=P(None, "rank", "tower"),
        check_vma=False,
    )
```

```python
import functools

import jax
import jax.numpy as jnp
from jax import lax
from jax.experimental import pallas as pl
from jax.experimental.pallas import tpu as pltpu
from jax.sharding import PartitionSpec as P

E = 128
CD = 128
CORES = 2
LINE = 4
PIECES = 2

epsilon = 1e-06
MESH = pl.DeviceIdType.MESH


def drain(ref, sem):
    pltpu.make_async_copy(ref, ref, sem).wait()


def fused(
    n_tower,
    n_rank,
    order_any,
    pooled,
    cross_w,
    cross_b,
    compress,
    gain,
    mlp_w,
    hid_b,
    hid_o,
    out,
    order,
    arrived,
    weights,
    compress_v,
    bias_v,
    flat_v,
    gain_v,
    bias_c,
    gain_c,
    first,
    state_a,
    state_b,
    towers,
    mixed,
    rows,
    packs,
    flat,
    hid_c,
    score,
    parts,
    aside,
    known,
    load_sem,
    a2a_send,
    a2a_recv,
    row_send,
    row_recv,
    pack_send,
    pack_recv,
    tower_send,
    tower_recv,
    mix_send,
    mix_recv,
    part_send,
    part_recv,
):
    micro = pooled.shape[0]
    block = arrived[0].shape[-1]
    layers, td = cross_w.shape[1], cross_w.shape[2]
    hid = mlp_w.shape[0]
    piece = hid // PIECES
    chunks = [(b, j) for b in range(micro) for j in range(CORES)]
    t = lax.axis_index("tower")
    r = lax.axis_index("rank")
    z = r // CORES
    c = lax.rem(r, CORES)
    mate = z * CORES + (1 - c)
    half = z // 2
    here, there = 1 + half, 2 - half
    near, far = 3 * half, 3 * (1 - half)
    inner = z == here
    outer = z != here
    steps = [1 << i for i in range(n_tower.bit_length() - 1)]

    barrier = pltpu.get_barrier_semaphore()

    def greet(**device):
        pl.semaphore_signal(barrier, inc=1, device_id=device, device_id_type=MESH)

    own_loads = [
        pltpu.make_async_copy(
            pooled.at[b, :, pl.ds(pl.multiple_of(((2 * half + c) * CORES + j) * block, block), block)],
            arrived[q].at[r],
            a2a_recv.at[q],
        )
        for q, (b, j) in enumerate(chunks)
    ]
    own_packs = [pltpu.make_async_copy(ref, packs.at[half, z % 2, i], pack_recv.at[0]) for i, ref in enumerate((hid_b, hid_o))]
    loads = [
        pltpu.make_async_copy(cross_b, bias_v, load_sem.at[0]),
        pltpu.make_async_copy(gain, gain_v, load_sem.at[0]),
        pltpu.make_async_copy(compress.at[0], compress_v, load_sem.at[0]),
        pltpu.make_async_copy(mlp_w, rows.at[half, pl.ds((z % 2) * hid, hid)], load_sem.at[0]),
        pltpu.make_async_copy(order_any, order, load_sem.at[0]),
    ]
    w_loads = [pltpu.make_async_copy(cross_w.at[0, l], weights.at[l], load_sem.at[1 + l]) for l in range(layers)]

    def send_block(q, chip, core):
        b, j = chunks[q]
        rank = ((chip // 2) * 2 + core) * CORES + j
        pltpu.make_async_remote_copy(
            src_ref=pooled.at[b, :, pl.ds(pl.multiple_of(rank * block, block), block)],
            dst_ref=arrived[q].at[r],
            send_sem=a2a_send.at[0],
            recv_sem=a2a_recv.at[q],
            device_id={"rank": chip * CORES + core},
            device_id_type=MESH,
        ).start()

    def send_rows(chip):
        for p in range(PIECES):
            pltpu.make_async_remote_copy(
                src_ref=mlp_w.at[pl.ds(p * piece, piece)],
                dst_ref=rows.at[half, pl.ds((z % 2) * hid + p * piece, piece)],
                send_sem=row_send.at[0],
                recv_sem=row_recv.at[z, p],
                device_id={"rank": chip * CORES + c},
                device_id_type=MESH,
            ).start()

    def send_packs(chip):
        for i, ref in enumerate((hid_b, hid_o)):
            pltpu.make_async_remote_copy(
                src_ref=ref,
                dst_ref=packs.at[half, z % 2, i],
                send_sem=pack_send.at[0],
                recv_sem=pack_recv.at[0],
                device_id={"rank": chip * CORES + c},
                device_id_type=MESH,
            ).start()

    @pl.when(outer)
    def _():
        pl.semaphore_wait(barrier, 2 * CORES)
        for q in range(len(chunks)):
            for chip in (there, here):
                for core in (c, 1 - c):
                    send_block(q, chip, core)
        for chip in (here, there):
            send_packs(chip)
        for chip in (here, there):
            send_rows(chip)

    width = block // n_tower

    def finish(count):
        drain(parts.at[:count], part_recv.at[0])
        logits = parts[0]
        for u in range(1, n_tower * CORES):
            logits = logits + parts[u]
        for u in range(n_tower):

            @pl.when(t == u)
            def _():
                for b in range(micro):
                    out[b] = logits[:, b * block + u * width : b * block + (u + 1) * width]

    @pl.when(inner)
    def _():
        for k in range(CORES):
            greet(rank=there * CORES + k)
        for k in range(CORES):
            greet(rank=far * CORES + k)
            greet(rank=near * CORES + k)
        greet(rank=mate)
        for d in steps:
            greet(tower=t ^ d)
        for copy in own_loads + own_packs + loads + w_loads:
            copy.start()
        pl.semaphore_wait(barrier, 2 * CORES - 1 + len(steps))
        if len(steps) > 1:
            pl.semaphore_signal(known.at[0], inc=1, device_id={"tower": t ^ 1}, device_id_type=MESH)
        for q in range(len(chunks)):
            for core in (c, 1 - c):
                send_block(q, there, core)
            send_block(q, here, 1 - c)
        send_packs(there)
        send_rows(there)

        for copy in loads:
            copy.wait()
        for l in range(layers):
            flat_v[l : l + 1, :] = bias_v[l]
        bias_c[...] = flat_v[...].T
        gain_c[...] = jnp.broadcast_to(gain_v[...], (8, CD)).T
        for q in range(len(chunks)):
            score[q] = jnp.zeros(score.shape[1:], jnp.float32)

        per_feature = n_rank // order.shape[1]
        height = arrived[0].shape[1]

        def tower(q):
            cols = slice(q * block, (q + 1) * block)
            drain(arrived[q], a2a_recv.at[q])
            for slot in range(order.shape[1]):
                feature = order[0, slot]
                for h in range(per_feature):
                    first[slot * E + h * height : slot * E + (h + 1) * height, cols] = arrived[q][
                        feature * per_feature + h
                    ]

            current, spare = first, state_a
            for l in range(layers):
                if q == 0:
                    w_loads[l].wait()
                for m in range(0, td, E):
                    at = slice(m, m + E)
                    product = (
                        jnp.dot(weights[l, at, :], current[:, cols], preferred_element_type=jnp.float32)
                        + bias_c[at, l : l + 1]
                    )
                    spare[at, cols] = (
                        first[at, cols].astype(jnp.float32) * product
                        + current[at, cols].astype(jnp.float32)
                    ).astype(jnp.bfloat16)
                current, spare = spare, (state_b if spare is state_a else state_a)
            squeezed = jnp.dot(compress_v[...], current[:, cols], preferred_element_type=jnp.float32)
            inverse_rms = lax.rsqrt(jnp.mean(squeezed * squeezed, axis=0, keepdims=True) + epsilon)
            towers[q][t] = (squeezed * inverse_rms * gain_c[:, 0:1]).astype(jnp.bfloat16)
            if q == 0 and len(steps) > 1:
                pl.semaphore_wait(known.at[0], 1)
            for d in range(n_tower - 1, 0, -1):
                pltpu.make_async_remote_copy(
                    src_ref=towers[q].at[t],
                    dst_ref=towers[q].at[t],
                    send_sem=tower_send.at[0],
                    recv_sem=tower_recv.at[q],
                    device_id={"tower": t ^ d},
                    device_id_type=MESH,
                ).start()

        def mix(q):
            drain(towers[q].at[: n_tower - 1], tower_recv.at[q])
            values = [towers[q][u].astype(jnp.float32) for u in range(n_tower)]
            gram = {}
            for u in range(n_tower):
                for v in range(u, n_tower):
                    gram[u, v] = gram[v, u] = jnp.sum(values[u] * values[v], axis=0, keepdims=True) / CD
            for u in range(n_tower):
                total = values[u]
                for v in range(n_tower):
                    total = total + gram[u, v] * values[v]
                mixed[q][u * CD : (u + 1) * CD, :block] = total.astype(jnp.bfloat16)
            pltpu.make_async_remote_copy(
                src_ref=mixed[q].at[:, pl.ds(0, block)],
                dst_ref=mixed[q].at[:, pl.ds(block, block)],
                send_sem=mix_send.at[0],
                recv_sem=mix_recv.at[q],
                device_id={"rank": mate},
                device_id_type=MESH,
            ).start()

        def mate_mixed(q):
            drain(mixed[q].at[:, pl.ds(block, block)], mix_recv.at[q])

        def landed(s, p):
            drain(rows.at[0, pl.ds(0, piece)], row_recv.at[s, p])

        def add(q, pair):
            hidden = jnp.dot(rows[pair], mixed[q][...], preferred_element_type=jnp.float32)
            bias, weight = hid_c[pair, 0], hid_c[pair, 1]
            for k in range(CORES):
                at = slice(k * block, (k + 1) * block)
                terms = jnp.maximum(hidden[:, at] + bias, 0.0) * weight
                score[q, :, at] = score[q, :, at] + jnp.sum(terms.reshape(-1, 8, block), axis=0)

        def prepare():
            drain(packs, pack_recv.at[0])
            for s in range(LINE):
                for i in range(2):
                    flat[2 * s + i : 2 * s + i + 1, :] = packs[s // 2, s % 2, i].astype(jnp.float32)
            turned = flat[...].T
            for s in range(LINE):
                for i in range(2):
                    hid_c[s // 2, i, (s % 2) * hid : (s % 2 + 1) * hid, :] = jnp.broadcast_to(
                        turned[:, 2 * s + i : 2 * s + i + 1], (hid, block)
                    )

        count = len(chunks)
        tower(0)
        tower(1)
        tower(2)
        mix(0)
        tower(3)
        mix(1)
        prepare()
        mix(2)
        for p in range(PIECES):
            landed(near, p)
        for q in range(2):
            mate_mixed(q)
            add(q, half)
        mix(3)
        mate_mixed(2)
        add(2, half)
        for s in (far, there):
            for p in range(PIECES):
                landed(s, p)
        for q in range(3):
            add(q, 1 - half)
        mate_mixed(3)
        add(3, half)
        add(3, 1 - half)

        me = t * CORES + c
        for q, (b, j) in enumerate(chunks):
            at = slice(b * block, (b + 1) * block)
            aside[c, j, :, at] = jnp.sum(score[q, :, :block], axis=0, keepdims=True)
            aside[1 - c, j, :, at] = jnp.sum(score[q, :, block:], axis=0, keepdims=True)
        for d in range(n_tower - 1, -1, -1):
            for k in (half, 1 - half):
                for j in range(CORES):
                    rank = (2 * half + k) * CORES + j

                    def hand_over(k=k, j=j, rank=rank, d=d):
                        pltpu.make_async_remote_copy(
                            src_ref=aside.at[k, j],
                            dst_ref=parts.at[me],
                            send_sem=part_send.at[0],
                            recv_sem=part_recv.at[0],
                            device_id={"tower": t ^ d, "rank": rank},
                            device_id_type=MESH,
                        ).start()

                    if d:
                        hand_over()
                    else:
                        pl.when(rank != r)(hand_over)
        parts[me] = aside[1 - half, c]

        for q in range(count):
            drain(arrived[q].at[:CORES + 1], a2a_send.at[0])
            drain(towers[q].at[: n_tower - 1], tower_send.at[0])
            drain(mixed[q].at[:, pl.ds(0, block)], mix_send.at[0])
        drain(packs.at[0, 0], pack_send.at[0])
        drain(rows.at[0, pl.ds(0, hid)], row_send.at[0])
        finish(n_tower * CORES - 1)
        drain(parts, part_send.at[0])
        drain(parts.at[: n_tower * CORES - 1], part_send.at[0])

    @pl.when(outer)
    def _():
        for q in range(len(chunks)):
            drain(arrived[q].at[: 2 * CORES], a2a_send.at[0])
        drain(packs.at[0], pack_send.at[0])
        drain(rows.at[0], row_send.at[0])
        finish(n_tower * CORES)


def in_one_kernel(
    n_tower, n_rank, pooled, order, cross_w, cross_b, compress, gain, mlp_w, mlp_bias, out_weight
):
    micro, height, samples = pooled.shape
    block = samples // n_rank
    _, layers, td, _ = cross_w.shape
    hid, width = mlp_w.shape
    chips = n_rank // CORES
    count = micro * CORES
    every = count * block
    bf16, f32 = jnp.bfloat16, jnp.float32
    dma = pltpu.SemaphoreType.DMA
    hbm = pl.BlockSpec(memory_space=pl.ANY)
    return pl.pallas_call(
        functools.partial(fused, n_tower, n_rank),
        out_shape=pltpu.VMEM((micro, 1, block // n_tower), f32),
        in_specs=[hbm] * 9,
        out_specs=pl.BlockSpec(memory_space=pltpu.VMEM),
        scratch_shapes=[
            pltpu.SMEM(order.shape, order.dtype),
            [pltpu.VMEM((n_rank, height, block), bf16)] * count,
            pltpu.VMEM((layers, td, td), bf16),
            pltpu.VMEM((CD, td), bf16),
            pltpu.VMEM((layers, 1, td), f32),
            pltpu.VMEM((8, td), f32),
            pltpu.VMEM((1, CD), f32),
            pltpu.VMEM((td, 8), f32),
            pltpu.VMEM((CD, 8), f32),
            pltpu.VMEM((td, every), bf16),
            pltpu.VMEM((td, every), bf16),
            pltpu.VMEM((td, every), bf16),
            [pltpu.VMEM((n_tower, CD, block), bf16)] * count,
            [pltpu.VMEM((width, CORES * block), bf16)] * count,
            pltpu.VMEM((2, 2 * hid, width), bf16),
            pltpu.VMEM((2, 2, 2, 1, hid), bf16),
            pltpu.VMEM((2 * chips, hid), f32),
            pltpu.VMEM((2, 2, 2 * hid, block), f32),
            pltpu.VMEM((count, 8, CORES * block), f32),
            pltpu.VMEM((n_tower * CORES, 1, micro * block), f32),
            pltpu.VMEM((CORES, CORES, 1, micro * block), f32),
            pltpu.SemaphoreType.REGULAR((1,)),
            dma((1 + layers,)),
            dma((1,)),
            dma((count,)),
            dma((1,)),
            dma((chips, PIECES)),
            dma((1,)),
            dma((1,)),
            dma((1,)),
            dma((count,)),
            dma((1,)),
            dma((count,)),
            dma((1,)),
            dma((1,)),
        ],
        compiler_params=pltpu.CompilerParams(collective_id=0, has_side_effects=True),
    )(
        order,
        pooled,
        cross_w,
        cross_b.swapaxes(0, 1),
        compress,
        gain,
        mlp_w,
        mlp_bias[None],
        out_weight[None],
    )


def tower_block(first, weights, biases, compress, gain):
    first_f = first.astype(jnp.float32)
    current = first
    for layer in range(weights.shape[0]):
        product = (
            jnp.dot(weights[layer], current, preferred_element_type=jnp.float32)
            + biases[layer][:, None]
        )
        current = (first_f * product + current.astype(jnp.float32)).astype(jnp.bfloat16)
    squeezed = jnp.dot(compress, current, preferred_element_type=jnp.float32)
    inverse_rms = lax.rsqrt(jnp.mean(squeezed * squeezed, axis=0, keepdims=True) + epsilon)
    return (squeezed * inverse_rms * gain[:, None]).astype(jnp.bfloat16)


def interact(joined):
    samples_now = joined.shape[1]
    values_f = joined.astype(jnp.float32).reshape(-1, CD, samples_now)
    gram = jnp.einsum("tck,uck->tuk", values_f, values_f, precision=lax.Precision.HIGHEST) / CD
    mixed = values_f + jnp.einsum("tuk,uck->tck", gram, values_f, precision=lax.Precision.HIGHEST)
    return mixed.reshape(-1, samples_now).astype(jnp.bfloat16)


def logit_terms(hidden_rows, hidden_bias, hidden_out, features):
    hidden = (
        jnp.dot(hidden_rows, features, preferred_element_type=jnp.float32)
        + hidden_bias.astype(jnp.float32)[:, None]
    )
    return jnp.sum(
        jax.nn.relu(hidden) * hidden_out.astype(jnp.float32)[:, None], axis=0, keepdims=True
    )


def by_collectives(
    pooled,
    feature_order,
    cross_weight,
    cross_bias,
    compress_weight,
    norm_gain,
    mlp_weight,
    mlp_bias,
    out_weight,
):
    micro_count = pooled.shape[0]
    arriving = [
        lax.all_to_all(pooled[batch], "rank", split_axis=1, concat_axis=0, tiled=True)
        for batch in range(micro_count)
    ]
    hidden_rows, hidden_bias, hidden_out = (
        lax.all_gather(mlp_weight, "rank", axis=0, tiled=True),
        lax.all_gather(mlp_bias, "rank", axis=0, tiled=True),
        lax.all_gather(out_weight, "rank", axis=0, tiled=True),
    )
    results = []
    for batch in range(micro_count):
        arrived = arriving[batch]
        samples_here = arrived.shape[1]
        first = jnp.take(arrived.reshape(-1, E, samples_here), feature_order[0], axis=0).reshape(
            -1, samples_here
        )
        compressed = tower_block(
            first, cross_weight[0], cross_bias[0], compress_weight[0], norm_gain[0]
        )
        all_towers = lax.all_gather(compressed, "tower", axis=0, tiled=True)
        partial_value = logit_terms(hidden_rows, hidden_bias, hidden_out, interact(all_towers))
        logit_row = lax.psum_scatter(partial_value, "tower", scatter_dimension=1, tiled=True)
        results.append(logit_row)
    return jnp.stack(results)


def fits(mesh, pooled, mlp_w):
    towers, ranks = mesh.shape["tower"], mesh.shape["rank"]
    height, hid = pooled.shape[1], mlp_w.shape[0]
    return (
        ranks == LINE * CORES
        and towers in (1, 2, 4)
        and pooled.shape[0] == 2
        and E % height == 0
        and height % 16 == 0
        and hid % 128 == 0
        and (pooled.shape[2] // ranks) % 128 == 0
    )


def solution(mesh):
    def on_device(*args):
        if fits(mesh, args[0], args[6]):
            return in_one_kernel(mesh.shape["tower"], mesh.shape["rank"], *args)
        return by_collectives(*args)

    return jax.shard_map(
        on_device,
        mesh=mesh,
        in_specs=(
            P(None, ("tower", "rank"), None),
            P("tower", None),
            P("tower", None, None, None),
            P("tower", None, None),
            P("tower", None, None),
            P("tower", None),
            P(("tower", "rank"), None),
            P(("tower", "rank")),
            P(("tower", "rank")),
        ),
        out_specs=P(None, "rank", "tower"),
        check_vma=False,
    )
```

```python
import functools

import jax
import jax.numpy as jnp
from jax import lax
from jax.experimental import pallas as pl
from jax.experimental.pallas import tpu as pltpu
from jax.sharding import PartitionSpec as P

E = 128
CD = 128
CORES = 2
LINE = 4

epsilon = 1e-06
MESH = pl.DeviceIdType.MESH


def drain(ref, sem):
    pltpu.make_async_copy(ref, ref, sem).wait()


def fused(
    n_tower,
    n_rank,
    order_any,
    pooled,
    cross_w,
    cross_b,
    compress,
    gain,
    mlp_w,
    hid_b,
    hid_o,
    out,
    order,
    arrived,
    weights,
    compress_v,
    bias_v,
    flat_v,
    gain_v,
    bias_c,
    gain_c,
    first,
    state_a,
    state_b,
    towers,
    mixed,
    rows,
    packs,
    flat,
    hid_c,
    score,
    parts,
    aside,
    known,
    load_sem,
    a2a_send,
    a2a_recv,
    row_send,
    row_recv,
    pack_send,
    pack_recv,
    tower_send,
    tower_recv,
    mix_send,
    mix_recv,
    part_send,
    part_recv,
):
    micro = pooled.shape[0]
    block = arrived[0].shape[-1]
    layers, td = cross_w.shape[1], cross_w.shape[2]
    hid = mlp_w.shape[0]
    chunks = [(b, j) for b in range(micro) for j in range(CORES)]
    t = lax.axis_index("tower")
    r = lax.axis_index("rank")
    z = r // CORES
    c = lax.rem(r, CORES)
    mate = z * CORES + (1 - c)
    half = z // 2
    here, there = 1 + half, 2 - half
    near, far = 3 * half, 3 * (1 - half)
    inner = z == here
    outer = z != here
    steps = [1 << i for i in range(n_tower.bit_length() - 1)]

    barrier = pltpu.get_barrier_semaphore()

    def greet(**device):
        pl.semaphore_signal(barrier, inc=1, device_id=device, device_id_type=MESH)

    own_loads = [
        pltpu.make_async_copy(
            pooled.at[b, :, pl.ds(pl.multiple_of(((2 * half + c) * CORES + j) * block, block), block)],
            arrived[q].at[r],
            a2a_recv.at[q],
        )
        for q, (b, j) in enumerate(chunks)
    ]
    own_packs = [pltpu.make_async_copy(ref, packs.at[half, z % 2, i], pack_recv.at[0]) for i, ref in enumerate((hid_b, hid_o))]
    loads = [
        pltpu.make_async_copy(cross_b, bias_v, load_sem.at[0]),
        pltpu.make_async_copy(gain, gain_v, load_sem.at[0]),
        pltpu.make_async_copy(compress.at[0], compress_v, load_sem.at[0]),
        pltpu.make_async_copy(mlp_w, rows.at[half, pl.ds((z % 2) * hid, hid)], load_sem.at[0]),
        pltpu.make_async_copy(order_any, order, load_sem.at[0]),
    ]
    w_loads = [pltpu.make_async_copy(cross_w.at[0, l], weights.at[l], load_sem.at[1 + l]) for l in range(layers)]

    def send_block(q, chip, core):
        b, j = chunks[q]
        rank = ((chip // 2) * 2 + core) * CORES + j
        pltpu.make_async_remote_copy(
            src_ref=pooled.at[b, :, pl.ds(pl.multiple_of(rank * block, block), block)],
            dst_ref=arrived[q].at[r],
            send_sem=a2a_send.at[0],
            recv_sem=a2a_recv.at[q],
            device_id={"rank": chip * CORES + core},
            device_id_type=MESH,
        ).start()

    def send_rows(chip, group):
        pltpu.make_async_remote_copy(
            src_ref=mlp_w,
            dst_ref=rows.at[half, pl.ds((z % 2) * hid, hid)],
            send_sem=row_send.at[0],
            recv_sem=row_recv.at[group],
            device_id={"rank": chip * CORES + c},
            device_id_type=MESH,
        ).start()

    def send_packs(chip):
        for i, ref in enumerate((hid_b, hid_o)):
            pltpu.make_async_remote_copy(
                src_ref=ref,
                dst_ref=packs.at[half, z % 2, i],
                send_sem=pack_send.at[0],
                recv_sem=pack_recv.at[0],
                device_id={"rank": chip * CORES + c},
                device_id_type=MESH,
            ).start()

    @pl.when(outer)
    def _():
        pl.semaphore_wait(barrier, 2 * CORES)
        for chip in (there, here):
            send_packs(chip)
        for q in range(len(chunks)):
            for chip in (there, here):
                for core in (c, 1 - c):
                    send_block(q, chip, core)
        send_rows(here, 0)
        send_rows(there, 1)

    width = block // n_tower

    def finish(count):
        drain(parts.at[:count], part_recv.at[0])
        logits = parts[0]
        for u in range(1, n_tower * CORES):
            logits = logits + parts[u]
        for u in range(n_tower):

            @pl.when(t == u)
            def _():
                for b in range(micro):
                    out[b] = logits[:, b * block + u * width : b * block + (u + 1) * width]

    @pl.when(inner)
    def _():
        for k in range(CORES):
            greet(rank=there * CORES + k)
        for k in range(CORES):
            greet(rank=far * CORES + k)
            greet(rank=near * CORES + k)
        greet(rank=mate)
        for d in steps:
            greet(tower=t ^ d)
        for copy in own_loads + own_packs + loads + w_loads:
            copy.start()
        pl.semaphore_wait(barrier, 2 * CORES - 1 + len(steps))
        if len(steps) > 1:
            pl.semaphore_signal(known.at[0], inc=1, device_id={"tower": t ^ 1}, device_id_type=MESH)
        send_packs(there)
        for q in range(len(chunks)):
            for core in (c, 1 - c):
                send_block(q, there, core)
            send_block(q, here, 1 - c)
        send_rows(there, 1)

        for copy in loads:
            copy.wait()
        for l in range(layers):
            flat_v[l : l + 1, :] = bias_v[l]
        bias_c[...] = flat_v[...].T
        gain_c[...] = jnp.broadcast_to(gain_v[...], (8, CD)).T
        for q in range(len(chunks)):
            score[q] = jnp.zeros(score.shape[1:], jnp.float32)

        per_feature = n_rank // order.shape[1]
        height = arrived[0].shape[1]

        def tower(q):
            cols = slice(q * block, (q + 1) * block)
            drain(arrived[q], a2a_recv.at[q])
            for slot in range(order.shape[1]):
                feature = order[0, slot]
                for h in range(per_feature):
                    first[slot * E + h * height : slot * E + (h + 1) * height, cols] = arrived[q][
                        feature * per_feature + h
                    ]

            current, spare = first, state_a
            for l in range(layers):
                if q == 0:
                    w_loads[l].wait()
                for m in range(0, td, E):
                    at = slice(m, m + E)
                    product = (
                        jnp.dot(weights[l, at, :], current[:, cols], preferred_element_type=jnp.float32)
                        + bias_c[at, l : l + 1]
                    )
                    spare[at, cols] = (
                        first[at, cols].astype(jnp.float32) * product
                        + current[at, cols].astype(jnp.float32)
                    ).astype(jnp.bfloat16)
                current, spare = spare, (state_b if spare is state_a else state_a)
            squeezed = jnp.dot(compress_v[...], current[:, cols], preferred_element_type=jnp.float32)
            inverse_rms = lax.rsqrt(jnp.mean(squeezed * squeezed, axis=0, keepdims=True) + epsilon)
            towers[q][t] = (squeezed * inverse_rms * gain_c[:, 0:1]).astype(jnp.bfloat16)
            if q == 0 and len(steps) > 1:
                pl.semaphore_wait(known.at[0], 1)
            for d in range(n_tower - 1, 0, -1):
                pltpu.make_async_remote_copy(
                    src_ref=towers[q].at[t],
                    dst_ref=towers[q].at[t],
                    send_sem=tower_send.at[0],
                    recv_sem=tower_recv.at[q],
                    device_id={"tower": t ^ d},
                    device_id_type=MESH,
                ).start()

        def mix(q):
            drain(towers[q].at[: n_tower - 1], tower_recv.at[q])
            values = [towers[q][u].astype(jnp.float32) for u in range(n_tower)]
            gram = {}
            for u in range(n_tower):
                for v in range(u, n_tower):
                    gram[u, v] = gram[v, u] = jnp.sum(values[u] * values[v], axis=0, keepdims=True) / CD
            for u in range(n_tower):
                total = values[u]
                for v in range(n_tower):
                    total = total + gram[u, v] * values[v]
                mixed[q][u * CD : (u + 1) * CD, :block] = total.astype(jnp.bfloat16)
            pltpu.make_async_remote_copy(
                src_ref=mixed[q].at[:, pl.ds(0, block)],
                dst_ref=mixed[q].at[:, pl.ds(block, block)],
                send_sem=mix_send.at[0],
                recv_sem=mix_recv.at[q],
                device_id={"rank": mate},
                device_id_type=MESH,
            ).start()

        def mate_mixed(q):
            drain(mixed[q].at[:, pl.ds(block, block)], mix_recv.at[q])

        def add(q, pair, sides=range(CORES)):
            cols = slice(sides[0] * block, (sides[-1] + 1) * block)
            hidden = jnp.dot(rows[pair], mixed[q][:, cols], preferred_element_type=jnp.float32)
            bias, weight = hid_c[pair, 0], hid_c[pair, 1]
            for i, k in enumerate(sides):
                at = slice(k * block, (k + 1) * block)
                terms = jnp.maximum(hidden[:, i * block : (i + 1) * block] + bias, 0.0) * weight
                score[q, :, at] = score[q, :, at] + jnp.sum(terms.reshape(-1, 8, block), axis=0)

        def prepare():
            drain(packs, pack_recv.at[0])
            for s in range(LINE):
                for i in range(2):
                    flat[2 * s + i : 2 * s + i + 1, :] = packs[s // 2, s % 2, i].astype(jnp.float32)
            turned = flat[...].T
            for s in range(LINE):
                for i in range(2):
                    hid_c[s // 2, i, (s % 2) * hid : (s % 2 + 1) * hid, :] = jnp.broadcast_to(
                        turned[:, 2 * s + i : 2 * s + i + 1], (hid, block)
                    )

        count = len(chunks)
        prepare()
        for q in range(count):
            tower(q)
        mix(0)
        mix(1)
        mix(2)
        drain(rows.at[0, pl.ds(0, hid)], row_recv.at[0])
        for q in range(2):
            mate_mixed(q)
            add(q, half)
        mix(3)
        mate_mixed(2)
        add(2, half)
        add(3, half, [0])
        drain(rows.at[0], row_recv.at[1])
        for q in range(3):
            add(q, 1 - half)
        add(3, 1 - half, [0])
        mate_mixed(3)
        add(3, half, [1])
        add(3, 1 - half, [1])

        me = t * CORES + c
        for q, (b, j) in enumerate(chunks):
            at = slice(b * block, (b + 1) * block)
            aside[c, j, :, at] = jnp.sum(score[q, :, :block], axis=0, keepdims=True)
            aside[1 - c, j, :, at] = jnp.sum(score[q, :, block:], axis=0, keepdims=True)
        for d in range(n_tower - 1, -1, -1):
            for k in (half, 1 - half):
                for j in range(CORES):
                    rank = (2 * half + k) * CORES + j

                    def hand_over(k=k, j=j, rank=rank, d=d):
                        pltpu.make_async_remote_copy(
                            src_ref=aside.at[k, j],
                            dst_ref=parts.at[me],
                            send_sem=part_send.at[0],
                            recv_sem=part_recv.at[0],
                            device_id={"tower": t ^ d, "rank": rank},
                            device_id_type=MESH,
                        ).start()

                    if d:
                        hand_over()
                    else:
                        pl.when(rank != r)(hand_over)
        parts[me] = aside[1 - half, c]

        for q in range(count):
            drain(arrived[q].at[:CORES + 1], a2a_send.at[0])
            drain(towers[q].at[: n_tower - 1], tower_send.at[0])
            drain(mixed[q].at[:, pl.ds(0, block)], mix_send.at[0])
        drain(packs.at[0, 0], pack_send.at[0])
        drain(rows.at[0, pl.ds(0, hid)], row_send.at[0])
        finish(n_tower * CORES - 1)
        drain(parts, part_send.at[0])
        drain(parts.at[: n_tower * CORES - 1], part_send.at[0])

    @pl.when(outer)
    def _():
        for q in range(len(chunks)):
            drain(arrived[q].at[: 2 * CORES], a2a_send.at[0])
        drain(packs.at[0], pack_send.at[0])
        drain(rows.at[0], row_send.at[0])
        finish(n_tower * CORES)


def in_one_kernel(
    n_tower, n_rank, pooled, order, cross_w, cross_b, compress, gain, mlp_w, mlp_bias, out_weight
):
    micro, height, samples = pooled.shape
    block = samples // n_rank
    _, layers, td, _ = cross_w.shape
    hid, width = mlp_w.shape
    chips = n_rank // CORES
    count = micro * CORES
    every = count * block
    bf16, f32 = jnp.bfloat16, jnp.float32
    dma = pltpu.SemaphoreType.DMA
    hbm = pl.BlockSpec(memory_space=pl.ANY)
    return pl.pallas_call(
        functools.partial(fused, n_tower, n_rank),
        out_shape=pltpu.VMEM((micro, 1, block // n_tower), f32),
        in_specs=[hbm] * 9,
        out_specs=pl.BlockSpec(memory_space=pltpu.VMEM),
        scratch_shapes=[
            pltpu.SMEM(order.shape, order.dtype),
            [pltpu.VMEM((n_rank, height, block), bf16)] * count,
            pltpu.VMEM((layers, td, td), bf16),
            pltpu.VMEM((CD, td), bf16),
            pltpu.VMEM((layers, 1, td), f32),
            pltpu.VMEM((8, td), f32),
            pltpu.VMEM((1, CD), f32),
            pltpu.VMEM((td, 8), f32),
            pltpu.VMEM((CD, 8), f32),
            pltpu.VMEM((td, every), bf16),
            pltpu.VMEM((td, every), bf16),
            pltpu.VMEM((td, every), bf16),
            [pltpu.VMEM((n_tower, CD, block), bf16)] * count,
            [pltpu.VMEM((width, CORES * block), bf16)] * count,
            pltpu.VMEM((2, 2 * hid, width), bf16),
            pltpu.VMEM((2, 2, 2, 1, hid), bf16),
            pltpu.VMEM((2 * chips, hid), f32),
            pltpu.VMEM((2, 2, 2 * hid, block), f32),
            pltpu.VMEM((count, 8, CORES * block), f32),
            pltpu.VMEM((n_tower * CORES, 1, micro * block), f32),
            pltpu.VMEM((CORES, CORES, 1, micro * block), f32),
            pltpu.SemaphoreType.REGULAR((1,)),
            dma((1 + layers,)),
            dma((1,)),
            dma((count,)),
            dma((1,)),
            dma((2,)),
            dma((1,)),
            dma((1,)),
            dma((1,)),
            dma((count,)),
            dma((1,)),
            dma((count,)),
            dma((1,)),
            dma((1,)),
        ],
        compiler_params=pltpu.CompilerParams(collective_id=0, has_side_effects=True),
    )(
        order,
        pooled,
        cross_w,
        cross_b.swapaxes(0, 1),
        compress,
        gain,
        mlp_w,
        mlp_bias[None],
        out_weight[None],
    )


def tower_block(first, weights, biases, compress, gain):
    first_f = first.astype(jnp.float32)
    current = first
    for layer in range(weights.shape[0]):
        product = (
            jnp.dot(weights[layer], current, preferred_element_type=jnp.float32)
            + biases[layer][:, None]
        )
        current = (first_f * product + current.astype(jnp.float32)).astype(jnp.bfloat16)
    squeezed = jnp.dot(compress, current, preferred_element_type=jnp.float32)
    inverse_rms = lax.rsqrt(jnp.mean(squeezed * squeezed, axis=0, keepdims=True) + epsilon)
    return (squeezed * inverse_rms * gain[:, None]).astype(jnp.bfloat16)


def interact(joined):
    samples_now = joined.shape[1]
    values_f = joined.astype(jnp.float32).reshape(-1, CD, samples_now)
    gram = jnp.einsum("tck,uck->tuk", values_f, values_f, precision=lax.Precision.HIGHEST) / CD
    mixed = values_f + jnp.einsum("tuk,uck->tck", gram, values_f, precision=lax.Precision.HIGHEST)
    return mixed.reshape(-1, samples_now).astype(jnp.bfloat16)


def logit_terms(hidden_rows, hidden_bias, hidden_out, features):
    hidden = (
        jnp.dot(hidden_rows, features, preferred_element_type=jnp.float32)
        + hidden_bias.astype(jnp.float32)[:, None]
    )
    return jnp.sum(
        jax.nn.relu(hidden) * hidden_out.astype(jnp.float32)[:, None], axis=0, keepdims=True
    )


def by_collectives(
    pooled,
    feature_order,
    cross_weight,
    cross_bias,
    compress_weight,
    norm_gain,
    mlp_weight,
    mlp_bias,
    out_weight,
):
    micro_count = pooled.shape[0]
    arriving = [
        lax.all_to_all(pooled[batch], "rank", split_axis=1, concat_axis=0, tiled=True)
        for batch in range(micro_count)
    ]
    hidden_rows, hidden_bias, hidden_out = (
        lax.all_gather(mlp_weight, "rank", axis=0, tiled=True),
        lax.all_gather(mlp_bias, "rank", axis=0, tiled=True),
        lax.all_gather(out_weight, "rank", axis=0, tiled=True),
    )
    results = []
    for batch in range(micro_count):
        arrived = arriving[batch]
        samples_here = arrived.shape[1]
        first = jnp.take(arrived.reshape(-1, E, samples_here), feature_order[0], axis=0).reshape(
            -1, samples_here
        )
        compressed = tower_block(
            first, cross_weight[0], cross_bias[0], compress_weight[0], norm_gain[0]
        )
        all_towers = lax.all_gather(compressed, "tower", axis=0, tiled=True)
        partial_value = logit_terms(hidden_rows, hidden_bias, hidden_out, interact(all_towers))
        logit_row = lax.psum_scatter(partial_value, "tower", scatter_dimension=1, tiled=True)
        results.append(logit_row)
    return jnp.stack(results)


def fits(mesh, pooled, mlp_w):
    towers, ranks = mesh.shape["tower"], mesh.shape["rank"]
    height, hid = pooled.shape[1], mlp_w.shape[0]
    return (
        ranks == LINE * CORES
        and towers in (1, 2, 4)
        and pooled.shape[0] == 2
        and E % height == 0
        and height % 16 == 0
        and hid % 128 == 0
        and (pooled.shape[2] // ranks) % 128 == 0
    )


def solution(mesh):
    def on_device(*args):
        if fits(mesh, args[0], args[6]):
            return in_one_kernel(mesh.shape["tower"], mesh.shape["rank"], *args)
        return by_collectives(*args)

    return jax.shard_map(
        on_device,
        mesh=mesh,
        in_specs=(
            P(None, ("tower", "rank"), None),
            P("tower", None),
            P("tower", None, None, None),
            P("tower", None, None),
            P("tower", None, None),
            P("tower", None),
            P(("tower", "rank"), None),
            P(("tower", "rank")),
            P(("tower", "rank")),
        ),
        out_specs=P(None, "rank", "tower"),
        check_vma=False,
    )
```

```python
import functools

import jax
import jax.numpy as jnp
from jax import lax
from jax.experimental import pallas as pl
from jax.experimental.pallas import tpu as pltpu
from jax.sharding import PartitionSpec as P

E = 128
CD = 128
CORES = 2
LINE = 4

epsilon = 1e-06
MESH = pl.DeviceIdType.MESH


def drain(ref, sem):
    pltpu.make_async_copy(ref, ref, sem).wait()


def fused(
    n_tower,
    n_rank,
    order_any,
    pooled,
    cross_w,
    cross_b,
    compress,
    gain,
    mlp_w,
    hid_b,
    hid_o,
    out,
    order,
    arrived,
    weights,
    compress_v,
    bias_v,
    flat_v,
    gain_v,
    bias_c,
    gain_c,
    first,
    state_a,
    state_b,
    towers,
    mixed,
    rows,
    packs,
    flat,
    hid_c,
    score,
    parts,
    aside,
    known,
    load_sem,
    a2a_send,
    a2a_recv,
    row_send,
    row_recv,
    pack_send,
    pack_recv,
    tower_send,
    tower_recv,
    mix_send,
    mix_recv,
    part_send,
    part_recv,
):
    micro = pooled.shape[0]
    block = arrived[0].shape[-1]
    layers, td = cross_w.shape[1], cross_w.shape[2]
    hid = mlp_w.shape[0]
    chunks = [(b, j) for b in range(micro) for j in range(CORES)]
    t = lax.axis_index("tower")
    r = lax.axis_index("rank")
    z = r // CORES
    c = lax.rem(r, CORES)
    mate = z * CORES + (1 - c)
    half = z // 2
    here, there = 1 + half, 2 - half
    near, far = 3 * half, 3 * (1 - half)
    inner = z == here
    outer = z != here
    steps = [1 << i for i in range(n_tower.bit_length() - 1)]

    barrier = pltpu.get_barrier_semaphore()

    def greet(**device):
        pl.semaphore_signal(barrier, inc=1, device_id=device, device_id_type=MESH)

    own_loads = [
        pltpu.make_async_copy(
            pooled.at[b, :, pl.ds(pl.multiple_of(((2 * half + c) * CORES + j) * block, block), block)],
            arrived[q].at[r],
            a2a_recv.at[q],
        )
        for q, (b, j) in enumerate(chunks)
    ]
    own_packs = [pltpu.make_async_copy(ref, packs.at[half, z % 2, i], pack_recv.at[0]) for i, ref in enumerate((hid_b, hid_o))]
    loads = [
        pltpu.make_async_copy(cross_b, bias_v, load_sem.at[0]),
        pltpu.make_async_copy(gain, gain_v, load_sem.at[0]),
        pltpu.make_async_copy(compress.at[0], compress_v, load_sem.at[0]),
        pltpu.make_async_copy(mlp_w, rows.at[half, pl.ds((z % 2) * hid, hid)], load_sem.at[0]),
        pltpu.make_async_copy(order_any, order, load_sem.at[0]),
    ]
    w_loads = [pltpu.make_async_copy(cross_w.at[0, l], weights.at[l], load_sem.at[1]) for l in range(layers)]

    def send_block(q, chip, core):
        b, j = chunks[q]
        rank = ((chip // 2) * 2 + core) * CORES + j
        pltpu.make_async_remote_copy(
            src_ref=pooled.at[b, :, pl.ds(pl.multiple_of(rank * block, block), block)],
            dst_ref=arrived[q].at[r],
            send_sem=a2a_send.at[0],
            recv_sem=a2a_recv.at[q],
            device_id={"rank": chip * CORES + core},
            device_id_type=MESH,
        ).start()

    def send_rows(chip, group):
        pltpu.make_async_remote_copy(
            src_ref=mlp_w,
            dst_ref=rows.at[half, pl.ds((z % 2) * hid, hid)],
            send_sem=row_send.at[0],
            recv_sem=row_recv.at[group],
            device_id={"rank": chip * CORES + c},
            device_id_type=MESH,
        ).start()

    def send_packs(chip):
        for i, ref in enumerate((hid_b, hid_o)):
            pltpu.make_async_remote_copy(
                src_ref=ref,
                dst_ref=packs.at[half, z % 2, i],
                send_sem=pack_send.at[0],
                recv_sem=pack_recv.at[0],
                device_id={"rank": chip * CORES + c},
                device_id_type=MESH,
            ).start()

    @pl.when(outer)
    def _():
        pl.semaphore_wait(barrier, 2 * CORES)
        for chip in (there, here):
            send_packs(chip)
        for q in range(len(chunks)):
            for chip in (there, here):
                for core in (c, 1 - c):
                    send_block(q, chip, core)
        send_rows(here, 0)
        send_rows(there, 1)

    width = block // n_tower

    def finish(count):
        drain(parts.at[:count], part_recv.at[0])
        logits = parts[0]
        for u in range(1, n_tower * CORES):
            logits = logits + parts[u]
        for u in range(n_tower):

            @pl.when(t == u)
            def _():
                for b in range(micro):
                    out[b] = logits[:, b * block + u * width : b * block + (u + 1) * width]

    @pl.when(inner)
    def _():
        for chip in (far, there, near):
            for k in range(CORES):
                greet(rank=chip * CORES + k)
        greet(rank=mate)
        for d in steps:
            greet(tower=t ^ d)
        for copy in own_loads + own_packs + loads + w_loads:
            copy.start()
        pl.semaphore_wait(barrier, 2 * CORES - 1 + len(steps))
        if len(steps) > 1:
            pl.semaphore_signal(known.at[0], inc=1, device_id={"tower": t ^ 1}, device_id_type=MESH)
        send_packs(there)
        for q in range(len(chunks)):
            for core in (c, 1 - c):
                send_block(q, there, core)
            send_block(q, here, 1 - c)
        send_rows(there, 1)

        for copy in loads:
            copy.wait()
        for l in range(layers):
            flat_v[l : l + 1, :] = bias_v[l]
        bias_c[...] = flat_v[...].T
        gain_c[...] = jnp.broadcast_to(gain_v[...], (8, CD)).T
        for q in range(len(chunks)):
            score[q] = jnp.zeros(score.shape[1:], jnp.float32)

        per_feature = n_rank // order.shape[1]
        height = arrived[0].shape[1]

        def tower(q):
            cols = slice(q * block, (q + 1) * block)
            drain(arrived[q], a2a_recv.at[q])
            for slot in range(order.shape[1]):
                feature = order[0, slot]
                for h in range(per_feature):
                    first[slot * E + h * height : slot * E + (h + 1) * height, cols] = arrived[q][
                        feature * per_feature + h
                    ]

            current, spare = first, state_a
            for l in range(layers):
                if q == 0 and l == 0:
                    for copy in w_loads:
                        copy.wait()
                for m in range(0, td, E):
                    at = slice(m, m + E)
                    product = (
                        jnp.dot(weights[l, at, :], current[:, cols], preferred_element_type=jnp.float32)
                        + bias_c[at, l : l + 1]
                    )
                    spare[at, cols] = (
                        first[at, cols].astype(jnp.float32) * product
                        + current[at, cols].astype(jnp.float32)
                    ).astype(jnp.bfloat16)
                current, spare = spare, (state_b if spare is state_a else state_a)
            squeezed = jnp.dot(compress_v[...], current[:, cols], preferred_element_type=jnp.float32)
            inverse_rms = lax.rsqrt(jnp.mean(squeezed * squeezed, axis=0, keepdims=True) + epsilon)
            towers[q][t] = (squeezed * inverse_rms * gain_c[:, 0:1]).astype(jnp.bfloat16)
            if q == 0 and len(steps) > 1:
                pl.semaphore_wait(known.at[0], 1)
            for d in range(n_tower - 1, 0, -1):
                pltpu.make_async_remote_copy(
                    src_ref=towers[q].at[t],
                    dst_ref=towers[q].at[t],
                    send_sem=tower_send.at[0],
                    recv_sem=tower_recv.at[q],
                    device_id={"tower": t ^ d},
                    device_id_type=MESH,
                ).start()

        def mix(q):
            drain(towers[q].at[: n_tower - 1], tower_recv.at[q])
            values = [towers[q][u].astype(jnp.float32) for u in range(n_tower)]
            gram = {}
            for u in range(n_tower):
                for v in range(u, n_tower):
                    gram[u, v] = gram[v, u] = jnp.sum(values[u] * values[v], axis=0, keepdims=True) / CD
            for u in range(n_tower):
                total = values[u]
                for v in range(n_tower):
                    total = total + gram[u, v] * values[v]
                mixed[q][u * CD : (u + 1) * CD, :block] = total.astype(jnp.bfloat16)
                if u % 2:
                    part = pl.ds((u - 1) * CD, 2 * CD)
                    pltpu.make_async_remote_copy(
                        src_ref=mixed[q].at[part, pl.ds(0, block)],
                        dst_ref=mixed[q].at[part, pl.ds(block, block)],
                        send_sem=mix_send.at[0],
                        recv_sem=mix_recv.at[q],
                        device_id={"rank": mate},
                        device_id_type=MESH,
                    ).start()

        def mate_mixed(q):
            drain(mixed[q].at[:, pl.ds(block, block)], mix_recv.at[q])

        def add(q, pair, sides=range(CORES)):
            cols = slice(sides[0] * block, (sides[-1] + 1) * block)
            hidden = jnp.dot(rows[pair], mixed[q][:, cols], preferred_element_type=jnp.float32)
            bias, weight = hid_c[pair, 0], hid_c[pair, 1]
            for i, k in enumerate(sides):
                at = slice(k * block, (k + 1) * block)
                terms = jnp.maximum(hidden[:, i * block : (i + 1) * block] + bias, 0.0) * weight
                score[q, :, at] = score[q, :, at] + jnp.sum(terms.reshape(-1, 8, block), axis=0)

        def prepare():
            drain(packs, pack_recv.at[0])
            for s in range(LINE):
                for i in range(2):
                    flat[2 * s + i : 2 * s + i + 1, :] = packs[s // 2, s % 2, i].astype(jnp.float32)
            turned = flat[...].T
            for s in range(LINE):
                for i in range(2):
                    hid_c[s // 2, i, (s % 2) * hid : (s % 2 + 1) * hid, :] = jnp.broadcast_to(
                        turned[:, 2 * s + i : 2 * s + i + 1], (hid, block)
                    )

        me = t * CORES + c

        def settle(side, j):
            k = c if side == 0 else 1 - c
            rank = (2 * half + k) * CORES + j
            for b in range(micro):
                at = slice(b * block, (b + 1) * block)
                cols = slice(side * block, (side + 1) * block)
                aside[k, j, :, at] = jnp.sum(score[b * CORES + j, :, cols], axis=0, keepdims=True)

            def hand_over(d):
                pltpu.make_async_remote_copy(
                    src_ref=aside.at[k, j],
                    dst_ref=parts.at[me],
                    send_sem=part_send.at[0],
                    recv_sem=part_recv.at[0],
                    device_id={"tower": t ^ d, "rank": rank},
                    device_id_type=MESH,
                ).start()

            for d in range(n_tower - 1, 0, -1):
                hand_over(d)
            pl.when(rank != r)(functools.partial(hand_over, 0))

        count = len(chunks)
        prepare()
        for q in range(count):
            tower(q)
        mix(0)
        mix(1)
        mix(2)
        drain(rows.at[0, pl.ds(0, hid)], row_recv.at[0])
        for q in range(2):
            mate_mixed(q)
            add(q, half)
        mix(3)
        mate_mixed(2)
        add(2, half)
        add(3, half, [0])
        drain(rows.at[0], row_recv.at[1])
        for q in range(3):
            add(q, 1 - half)
        add(3, 1 - half, [0])
        for side, j in ((1, 0), (0, 0), (0, 1)):
            settle(side, j)
        mate_mixed(3)
        add(3, half, [1])
        add(3, 1 - half, [1])
        settle(1, 1)

        parts[me] = aside[1 - half, c]

        for q in range(count):
            drain(arrived[q].at[:CORES + 1], a2a_send.at[0])
            drain(towers[q].at[: n_tower - 1], tower_send.at[0])
            drain(mixed[q].at[:, pl.ds(0, block)], mix_send.at[0])
        drain(packs.at[0, 0], pack_send.at[0])
        drain(rows.at[0, pl.ds(0, hid)], row_send.at[0])
        finish(n_tower * CORES - 1)
        drain(parts, part_send.at[0])
        drain(parts.at[: n_tower * CORES - 1], part_send.at[0])

    @pl.when(outer)
    def _():
        for q in range(len(chunks)):
            drain(arrived[q].at[: 2 * CORES], a2a_send.at[0])
        drain(packs.at[0], pack_send.at[0])
        drain(rows.at[0], row_send.at[0])
        finish(n_tower * CORES)


def in_one_kernel(
    n_tower, n_rank, pooled, order, cross_w, cross_b, compress, gain, mlp_w, mlp_bias, out_weight
):
    micro, height, samples = pooled.shape
    block = samples // n_rank
    _, layers, td, _ = cross_w.shape
    hid, width = mlp_w.shape
    chips = n_rank // CORES
    count = micro * CORES
    every = count * block
    bf16, f32 = jnp.bfloat16, jnp.float32
    dma = pltpu.SemaphoreType.DMA
    hbm = pl.BlockSpec(memory_space=pl.ANY)
    return pl.pallas_call(
        functools.partial(fused, n_tower, n_rank),
        out_shape=pltpu.VMEM((micro, 1, block // n_tower), f32),
        in_specs=[hbm] * 9,
        out_specs=pl.BlockSpec(memory_space=pltpu.VMEM),
        scratch_shapes=[
            pltpu.SMEM(order.shape, order.dtype),
            [pltpu.VMEM((n_rank, height, block), bf16)] * count,
            pltpu.VMEM((layers, td, td), bf16),
            pltpu.VMEM((CD, td), bf16),
            pltpu.VMEM((layers, 1, td), f32),
            pltpu.VMEM((8, td), f32),
            pltpu.VMEM((1, CD), f32),
            pltpu.VMEM((td, 8), f32),
            pltpu.VMEM((CD, 8), f32),
            pltpu.VMEM((td, every), bf16),
            pltpu.VMEM((td, every), bf16),
            pltpu.VMEM((td, every), bf16),
            [pltpu.VMEM((n_tower, CD, block), bf16)] * count,
            [pltpu.VMEM((width, CORES * block), bf16)] * count,
            pltpu.VMEM((2, 2 * hid, width), bf16),
            pltpu.VMEM((2, 2, 2, 1, hid), bf16),
            pltpu.VMEM((2 * chips, hid), f32),
            pltpu.VMEM((2, 2, 2 * hid, block), f32),
            pltpu.VMEM((count, 8, CORES * block), f32),
            pltpu.VMEM((n_tower * CORES, 1, micro * block), f32),
            pltpu.VMEM((CORES, CORES, 1, micro * block), f32),
            pltpu.SemaphoreType.REGULAR((1,)),
            dma((2,)),
            dma((1,)),
            dma((count,)),
            dma((1,)),
            dma((2,)),
            dma((1,)),
            dma((1,)),
            dma((1,)),
            dma((count,)),
            dma((1,)),
            dma((count,)),
            dma((1,)),
            dma((1,)),
        ],
        compiler_params=pltpu.CompilerParams(collective_id=0, has_side_effects=True),
    )(
        order,
        pooled,
        cross_w,
        cross_b.swapaxes(0, 1),
        compress,
        gain,
        mlp_w,
        mlp_bias[None],
        out_weight[None],
    )


def tower_block(first, weights, biases, compress, gain):
    first_f = first.astype(jnp.float32)
    current = first
    for layer in range(weights.shape[0]):
        product = (
            jnp.dot(weights[layer], current, preferred_element_type=jnp.float32)
            + biases[layer][:, None]
        )
        current = (first_f * product + current.astype(jnp.float32)).astype(jnp.bfloat16)
    squeezed = jnp.dot(compress, current, preferred_element_type=jnp.float32)
    inverse_rms = lax.rsqrt(jnp.mean(squeezed * squeezed, axis=0, keepdims=True) + epsilon)
    return (squeezed * inverse_rms * gain[:, None]).astype(jnp.bfloat16)


def interact(joined):
    samples_now = joined.shape[1]
    values_f = joined.astype(jnp.float32).reshape(-1, CD, samples_now)
    gram = jnp.einsum("tck,uck->tuk", values_f, values_f, precision=lax.Precision.HIGHEST) / CD
    mixed = values_f + jnp.einsum("tuk,uck->tck", gram, values_f, precision=lax.Precision.HIGHEST)
    return mixed.reshape(-1, samples_now).astype(jnp.bfloat16)


def logit_terms(hidden_rows, hidden_bias, hidden_out, features):
    hidden = (
        jnp.dot(hidden_rows, features, preferred_element_type=jnp.float32)
        + hidden_bias.astype(jnp.float32)[:, None]
    )
    return jnp.sum(
        jax.nn.relu(hidden) * hidden_out.astype(jnp.float32)[:, None], axis=0, keepdims=True
    )


def by_collectives(
    pooled,
    feature_order,
    cross_weight,
    cross_bias,
    compress_weight,
    norm_gain,
    mlp_weight,
    mlp_bias,
    out_weight,
):
    micro_count = pooled.shape[0]
    arriving = [
        lax.all_to_all(pooled[batch], "rank", split_axis=1, concat_axis=0, tiled=True)
        for batch in range(micro_count)
    ]
    hidden_rows, hidden_bias, hidden_out = (
        lax.all_gather(mlp_weight, "rank", axis=0, tiled=True),
        lax.all_gather(mlp_bias, "rank", axis=0, tiled=True),
        lax.all_gather(out_weight, "rank", axis=0, tiled=True),
    )
    results = []
    for batch in range(micro_count):
        arrived = arriving[batch]
        samples_here = arrived.shape[1]
        first = jnp.take(arrived.reshape(-1, E, samples_here), feature_order[0], axis=0).reshape(
            -1, samples_here
        )
        compressed = tower_block(
            first, cross_weight[0], cross_bias[0], compress_weight[0], norm_gain[0]
        )
        all_towers = lax.all_gather(compressed, "tower", axis=0, tiled=True)
        partial_value = logit_terms(hidden_rows, hidden_bias, hidden_out, interact(all_towers))
        logit_row = lax.psum_scatter(partial_value, "tower", scatter_dimension=1, tiled=True)
        results.append(logit_row)
    return jnp.stack(results)


def fits(mesh, pooled, mlp_w):
    towers, ranks = mesh.shape["tower"], mesh.shape["rank"]
    height, hid = pooled.shape[1], mlp_w.shape[0]
    return (
        ranks == LINE * CORES
        and towers in (1, 2, 4)
        and pooled.shape[0] == 2
        and E % height == 0
        and height % 16 == 0
        and hid % 128 == 0
        and (pooled.shape[2] // ranks) % 128 == 0
    )


def solution(mesh):
    def on_device(*args):
        if fits(mesh, args[0], args[6]):
            return in_one_kernel(mesh.shape["tower"], mesh.shape["rank"], *args)
        return by_collectives(*args)

    return jax.shard_map(
        on_device,
        mesh=mesh,
        in_specs=(
            P(None, ("tower", "rank"), None),
            P("tower", None),
            P("tower", None, None, None),
            P("tower", None, None),
            P("tower", None, None),
            P("tower", None),
            P(("tower", "rank"), None),
            P(("tower", "rank")),
            P(("tower", "rank")),
        ),
        out_specs=P(None, "rank", "tower"),
        check_vma=False,
    )
```

```python
import functools

import jax
import jax.numpy as jnp
from jax import lax
from jax.experimental import pallas as pl
from jax.experimental.pallas import tpu as pltpu
from jax.sharding import PartitionSpec as P

E = 128
CD = 128
CORES = 2
LINE = 4

epsilon = 1e-06
MESH = pl.DeviceIdType.MESH


def drain(ref, sem):
    pltpu.make_async_copy(ref, ref, sem).wait()


def fused(
    n_tower,
    n_rank,
    order_any,
    pooled,
    cross_w,
    cross_b,
    compress,
    gain,
    mlp_w,
    hid_b,
    hid_o,
    out,
    order,
    arrived,
    weights,
    compress_v,
    bias_v,
    flat_v,
    gain_v,
    bias_c,
    gain_c,
    first,
    state_a,
    state_b,
    towers,
    mixed,
    rows,
    packs,
    flat,
    hid_c,
    score,
    parts,
    aside,
    known,
    load_sem,
    a2a_send,
    a2a_recv,
    row_send,
    row_recv,
    pack_send,
    pack_recv,
    tower_send,
    tower_recv,
    mix_send,
    mix_recv,
    part_send,
    part_recv,
):
    micro = pooled.shape[0]
    block = arrived[0].shape[-1]
    layers, td = cross_w.shape[1], cross_w.shape[2]
    hid = mlp_w.shape[0]
    chunks = [(b, j) for b in range(micro) for j in range(CORES)]
    t = lax.axis_index("tower")
    r = lax.axis_index("rank")
    z = r // CORES
    c = lax.rem(r, CORES)
    mate = z * CORES + (1 - c)
    half = z // 2
    here, there = 1 + half, 2 - half
    near, far = 3 * half, 3 * (1 - half)
    inner = z == here
    outer = z != here
    steps = [1 << i for i in range(n_tower.bit_length() - 1)]

    barrier = pltpu.get_barrier_semaphore()

    def greet(**device):
        pl.semaphore_signal(barrier, inc=1, device_id=device, device_id_type=MESH)

    own_loads = [
        pltpu.make_async_copy(
            pooled.at[b, :, pl.ds(pl.multiple_of(((2 * half + c) * CORES + j) * block, block), block)],
            arrived[q].at[r],
            a2a_recv.at[q],
        )
        for q, (b, j) in enumerate(chunks)
    ]
    own_packs = [pltpu.make_async_copy(ref, packs.at[half, z % 2, i], pack_recv.at[0]) for i, ref in enumerate((hid_b, hid_o))]
    loads = [
        pltpu.make_async_copy(cross_b, bias_v, load_sem.at[0]),
        pltpu.make_async_copy(gain, gain_v, load_sem.at[0]),
        pltpu.make_async_copy(compress.at[0], compress_v, load_sem.at[0]),
        pltpu.make_async_copy(mlp_w, rows.at[half, pl.ds((z % 2) * hid, hid)], load_sem.at[0]),
        pltpu.make_async_copy(order_any, order, load_sem.at[0]),
    ]
    w_loads = [pltpu.make_async_copy(cross_w.at[0, l], weights.at[l], load_sem.at[1]) for l in range(layers)]

    def send_block(q, chip, core):
        b, j = chunks[q]
        rank = ((chip // 2) * 2 + core) * CORES + j
        pltpu.make_async_remote_copy(
            src_ref=pooled.at[b, :, pl.ds(pl.multiple_of(rank * block, block), block)],
            dst_ref=arrived[q].at[r],
            send_sem=a2a_send.at[0],
            recv_sem=a2a_recv.at[q],
            device_id={"rank": chip * CORES + core},
            device_id_type=MESH,
        ).start()

    def send_rows(chip, group):
        pltpu.make_async_remote_copy(
            src_ref=mlp_w,
            dst_ref=rows.at[half, pl.ds((z % 2) * hid, hid)],
            send_sem=row_send.at[0],
            recv_sem=row_recv.at[group],
            device_id={"rank": chip * CORES + c},
            device_id_type=MESH,
        ).start()

    def send_packs(chip):
        for i, ref in enumerate((hid_b, hid_o)):
            pltpu.make_async_remote_copy(
                src_ref=ref,
                dst_ref=packs.at[half, z % 2, i],
                send_sem=pack_send.at[0],
                recv_sem=pack_recv.at[0],
                device_id={"rank": chip * CORES + c},
                device_id_type=MESH,
            ).start()

    @pl.when(outer)
    def _():
        pl.semaphore_wait(barrier, 2 * CORES)
        for chip in (there, here):
            send_packs(chip)
        for q in range(len(chunks)):
            for chip in (there, here):
                for core in (c, 1 - c):
                    send_block(q, chip, core)
        send_rows(here, 0)
        send_rows(there, 2)

    width = block // n_tower

    def finish(count):
        drain(parts.at[:count], part_recv.at[0])
        logits = parts[0]
        for u in range(1, n_tower * CORES):
            logits = logits + parts[u]
        for u in range(n_tower):

            @pl.when(t == u)
            def _():
                for b in range(micro):
                    out[b] = logits[:, b * block + u * width : b * block + (u + 1) * width]

    @pl.when(inner)
    def _():
        for chip in (far, there, near):
            for k in range(CORES):
                greet(rank=chip * CORES + k)
        greet(rank=mate)
        for d in steps:
            greet(tower=t ^ d)
        for copy in own_loads + own_packs + loads + w_loads:
            copy.start()
        pl.semaphore_wait(barrier, 2 * CORES - 1 + len(steps))
        if len(steps) > 1:
            pl.semaphore_signal(known.at[0], inc=1, device_id={"tower": t ^ 1}, device_id_type=MESH)
        send_packs(there)
        for q in range(len(chunks)):
            for core in (c, 1 - c):
                send_block(q, there, core)
            send_block(q, here, 1 - c)
        send_rows(there, 1)

        for copy in loads:
            copy.wait()
        for l in range(layers):
            flat_v[l : l + 1, :] = bias_v[l]
        bias_c[...] = flat_v[...].T
        gain_c[...] = jnp.broadcast_to(gain_v[...], (8, CD)).T
        for q in range(len(chunks)):
            score[q] = jnp.zeros(score.shape[1:], jnp.float32)

        per_feature = n_rank // order.shape[1]
        height = arrived[0].shape[1]

        def tower(q):
            cols = slice(q * block, (q + 1) * block)
            drain(arrived[q], a2a_recv.at[q])
            for slot in range(order.shape[1]):
                feature = order[0, slot]
                for h in range(per_feature):
                    first[slot * E + h * height : slot * E + (h + 1) * height, cols] = arrived[q][
                        feature * per_feature + h
                    ]

            current, spare = first, state_a
            for l in range(layers):
                if q == 0 and l == 0:
                    for copy in w_loads:
                        copy.wait()
                for m in range(0, td, E):
                    at = slice(m, m + E)
                    product = (
                        jnp.dot(weights[l, at, :], current[:, cols], preferred_element_type=jnp.float32)
                        + bias_c[at, l : l + 1]
                    )
                    spare[at, cols] = (
                        first[at, cols].astype(jnp.float32) * product
                        + current[at, cols].astype(jnp.float32)
                    ).astype(jnp.bfloat16)
                current, spare = spare, (state_b if spare is state_a else state_a)
            squeezed = jnp.dot(compress_v[...], current[:, cols], preferred_element_type=jnp.float32)
            inverse_rms = lax.rsqrt(jnp.mean(squeezed * squeezed, axis=0, keepdims=True) + epsilon)
            towers[q][t] = (squeezed * inverse_rms * gain_c[:, 0:1]).astype(jnp.bfloat16)
            if q == 0 and len(steps) > 1:
                pl.semaphore_wait(known.at[0], 1)
            for d in range(n_tower - 1, 0, -1):
                pltpu.make_async_remote_copy(
                    src_ref=towers[q].at[t],
                    dst_ref=towers[q].at[t],
                    send_sem=tower_send.at[0],
                    recv_sem=tower_recv.at[q],
                    device_id={"tower": t ^ d},
                    device_id_type=MESH,
                ).start()

        def mix(q):
            drain(towers[q].at[: n_tower - 1], tower_recv.at[q])
            values = [towers[q][u].astype(jnp.float32) for u in range(n_tower)]
            gram = {}
            for u in range(n_tower):
                for v in range(u, n_tower):
                    gram[u, v] = gram[v, u] = jnp.sum(values[u] * values[v], axis=0, keepdims=True) / CD
            for u in range(n_tower):
                total = values[u]
                for v in range(n_tower):
                    total = total + gram[u, v] * values[v]
                mixed[q][u * CD : (u + 1) * CD, :block] = total.astype(jnp.bfloat16)
                if u % 2:
                    part = pl.ds((u - 1) * CD, 2 * CD)
                    pltpu.make_async_remote_copy(
                        src_ref=mixed[q].at[part, pl.ds(0, block)],
                        dst_ref=mixed[q].at[part, pl.ds(block, block)],
                        send_sem=mix_send.at[0],
                        recv_sem=mix_recv.at[q],
                        device_id={"rank": mate},
                        device_id_type=MESH,
                    ).start()

        def mate_mixed(q):
            drain(mixed[q].at[:, pl.ds(block, block)], mix_recv.at[q])

        def add(q, pair, sides=range(CORES)):
            cols = slice(sides[0] * block, (sides[-1] + 1) * block)
            hidden = jnp.dot(rows[pair], mixed[q][:, cols], preferred_element_type=jnp.float32)
            bias, weight = hid_c[pair, 0], hid_c[pair, 1]
            for i, k in enumerate(sides):
                at = slice(k * block, (k + 1) * block)
                terms = jnp.maximum(hidden[:, i * block : (i + 1) * block] + bias, 0.0) * weight
                score[q, :, at] = score[q, :, at] + jnp.sum(terms.reshape(-1, 8, block), axis=0)

        def add_one(q, chip):
            here_rows = pl.ds(pl.multiple_of((chip % 2) * hid, hid), hid)
            hidden = jnp.dot(rows[1 - half, here_rows, :], mixed[q][...], preferred_element_type=jnp.float32)
            bias, weight = hid_c[1 - half, 0, here_rows, :], hid_c[1 - half, 1, here_rows, :]
            for k in range(CORES):
                at = slice(k * block, (k + 1) * block)
                terms = jnp.maximum(hidden[:, at] + bias, 0.0) * weight
                score[q, :, at] = score[q, :, at] + jnp.sum(terms.reshape(-1, 8, block), axis=0)

        def prepare():
            drain(packs, pack_recv.at[0])
            for s in range(LINE):
                for i in range(2):
                    flat[2 * s + i : 2 * s + i + 1, :] = packs[s // 2, s % 2, i].astype(jnp.float32)
            turned = flat[...].T
            for s in range(LINE):
                for i in range(2):
                    hid_c[s // 2, i, (s % 2) * hid : (s % 2 + 1) * hid, :] = jnp.broadcast_to(
                        turned[:, 2 * s + i : 2 * s + i + 1], (hid, block)
                    )

        me = t * CORES + c

        def settle(side, j):
            k = c if side == 0 else 1 - c
            rank = (2 * half + k) * CORES + j
            for b in range(micro):
                at = slice(b * block, (b + 1) * block)
                cols = slice(side * block, (side + 1) * block)
                aside[k, j, :, at] = jnp.sum(score[b * CORES + j, :, cols], axis=0, keepdims=True)

            def hand_over(d):
                pltpu.make_async_remote_copy(
                    src_ref=aside.at[k, j],
                    dst_ref=parts.at[me],
                    send_sem=part_send.at[0],
                    recv_sem=part_recv.at[0],
                    device_id={"tower": t ^ d, "rank": rank},
                    device_id_type=MESH,
                ).start()

            for d in range(n_tower - 1, 0, -1):
                hand_over(d)
            pl.when(rank != r)(functools.partial(hand_over, 0))

        count = len(chunks)
        prepare()
        for q in range(count):
            tower(q)
        mix(0)
        mix(1)
        mix(2)
        drain(rows.at[0, pl.ds(0, hid)], row_recv.at[0])
        for q in range(2):
            mate_mixed(q)
            add(q, half)
        mix(3)
        mate_mixed(2)
        add(2, half)
        add(3, half, [0])
        drain(rows.at[0, pl.ds(0, hid)], row_recv.at[1])
        for q in range(3):
            add_one(q, there)
        drain(rows.at[0, pl.ds(0, hid)], row_recv.at[2])
        add_one(0, far)
        add_one(2, far)
        settle(1, 0)
        settle(0, 0)
        add_one(1, far)
        add(3, 1 - half, [0])
        settle(0, 1)
        mate_mixed(3)
        add(3, half, [1])
        add(3, 1 - half, [1])
        settle(1, 1)

        parts[me] = aside[1 - half, c]

        for q in range(count):
            drain(arrived[q].at[:CORES + 1], a2a_send.at[0])
            drain(towers[q].at[: n_tower - 1], tower_send.at[0])
            drain(mixed[q].at[:, pl.ds(0, block)], mix_send.at[0])
        drain(packs.at[0, 0], pack_send.at[0])
        drain(rows.at[0, pl.ds(0, hid)], row_send.at[0])
        finish(n_tower * CORES - 1)
        drain(parts, part_send.at[0])
        drain(parts.at[: n_tower * CORES - 1], part_send.at[0])

    @pl.when(outer)
    def _():
        for q in range(len(chunks)):
            drain(arrived[q].at[: 2 * CORES], a2a_send.at[0])
        drain(packs.at[0], pack_send.at[0])
        drain(rows.at[0], row_send.at[0])
        finish(n_tower * CORES)


def in_one_kernel(
    n_tower, n_rank, pooled, order, cross_w, cross_b, compress, gain, mlp_w, mlp_bias, out_weight
):
    micro, height, samples = pooled.shape
    block = samples // n_rank
    _, layers, td, _ = cross_w.shape
    hid, width = mlp_w.shape
    chips = n_rank // CORES
    count = micro * CORES
    every = count * block
    bf16, f32 = jnp.bfloat16, jnp.float32
    dma = pltpu.SemaphoreType.DMA
    hbm = pl.BlockSpec(memory_space=pl.ANY)
    return pl.pallas_call(
        functools.partial(fused, n_tower, n_rank),
        out_shape=pltpu.VMEM((micro, 1, block // n_tower), f32),
        in_specs=[hbm] * 9,
        out_specs=pl.BlockSpec(memory_space=pltpu.VMEM),
        scratch_shapes=[
            pltpu.SMEM(order.shape, order.dtype),
            [pltpu.VMEM((n_rank, height, block), bf16)] * count,
            pltpu.VMEM((layers, td, td), bf16),
            pltpu.VMEM((CD, td), bf16),
            pltpu.VMEM((layers, 1, td), f32),
            pltpu.VMEM((8, td), f32),
            pltpu.VMEM((1, CD), f32),
            pltpu.VMEM((td, 8), f32),
            pltpu.VMEM((CD, 8), f32),
            pltpu.VMEM((td, every), bf16),
            pltpu.VMEM((td, every), bf16),
            pltpu.VMEM((td, every), bf16),
            [pltpu.VMEM((n_tower, CD, block), bf16)] * count,
            [pltpu.VMEM((width, CORES * block), bf16)] * count,
            pltpu.VMEM((2, 2 * hid, width), bf16),
            pltpu.VMEM((2, 2, 2, 1, hid), bf16),
            pltpu.VMEM((2 * chips, hid), f32),
            pltpu.VMEM((2, 2, 2 * hid, block), f32),
            pltpu.VMEM((count, 8, CORES * block), f32),
            pltpu.VMEM((n_tower * CORES, 1, micro * block), f32),
            pltpu.VMEM((CORES, CORES, 1, micro * block), f32),
            pltpu.SemaphoreType.REGULAR((1,)),
            dma((2,)),
            dma((1,)),
            dma((count,)),
            dma((1,)),
            dma((3,)),
            dma((1,)),
            dma((1,)),
            dma((1,)),
            dma((count,)),
            dma((1,)),
            dma((count,)),
            dma((1,)),
            dma((1,)),
        ],
        compiler_params=pltpu.CompilerParams(collective_id=0, has_side_effects=True),
    )(
        order,
        pooled,
        cross_w,
        cross_b.swapaxes(0, 1),
        compress,
        gain,
        mlp_w,
        mlp_bias[None],
        out_weight[None],
    )


def tower_block(first, weights, biases, compress, gain):
    first_f = first.astype(jnp.float32)
    current = first
    for layer in range(weights.shape[0]):
        product = (
            jnp.dot(weights[layer], current, preferred_element_type=jnp.float32)
            + biases[layer][:, None]
        )
        current = (first_f * product + current.astype(jnp.float32)).astype(jnp.bfloat16)
    squeezed = jnp.dot(compress, current, preferred_element_type=jnp.float32)
    inverse_rms = lax.rsqrt(jnp.mean(squeezed * squeezed, axis=0, keepdims=True) + epsilon)
    return (squeezed * inverse_rms * gain[:, None]).astype(jnp.bfloat16)


def interact(joined):
    samples_now = joined.shape[1]
    values_f = joined.astype(jnp.float32).reshape(-1, CD, samples_now)
    gram = jnp.einsum("tck,uck->tuk", values_f, values_f, precision=lax.Precision.HIGHEST) / CD
    mixed = values_f + jnp.einsum("tuk,uck->tck", gram, values_f, precision=lax.Precision.HIGHEST)
    return mixed.reshape(-1, samples_now).astype(jnp.bfloat16)


def logit_terms(hidden_rows, hidden_bias, hidden_out, features):
    hidden = (
        jnp.dot(hidden_rows, features, preferred_element_type=jnp.float32)
        + hidden_bias.astype(jnp.float32)[:, None]
    )
    return jnp.sum(
        jax.nn.relu(hidden) * hidden_out.astype(jnp.float32)[:, None], axis=0, keepdims=True
    )


def by_collectives(
    pooled,
    feature_order,
    cross_weight,
    cross_bias,
    compress_weight,
    norm_gain,
    mlp_weight,
    mlp_bias,
    out_weight,
):
    micro_count = pooled.shape[0]
    arriving = [
        lax.all_to_all(pooled[batch], "rank", split_axis=1, concat_axis=0, tiled=True)
        for batch in range(micro_count)
    ]
    hidden_rows, hidden_bias, hidden_out = (
        lax.all_gather(mlp_weight, "rank", axis=0, tiled=True),
        lax.all_gather(mlp_bias, "rank", axis=0, tiled=True),
        lax.all_gather(out_weight, "rank", axis=0, tiled=True),
    )
    results = []
    for batch in range(micro_count):
        arrived = arriving[batch]
        samples_here = arrived.shape[1]
        first = jnp.take(arrived.reshape(-1, E, samples_here), feature_order[0], axis=0).reshape(
            -1, samples_here
        )
        compressed = tower_block(
            first, cross_weight[0], cross_bias[0], compress_weight[0], norm_gain[0]
        )
        all_towers = lax.all_gather(compressed, "tower", axis=0, tiled=True)
        partial_value = logit_terms(hidden_rows, hidden_bias, hidden_out, interact(all_towers))
        logit_row = lax.psum_scatter(partial_value, "tower", scatter_dimension=1, tiled=True)
        results.append(logit_row)
    return jnp.stack(results)


def fits(mesh, pooled, mlp_w):
    towers, ranks = mesh.shape["tower"], mesh.shape["rank"]
    height, hid = pooled.shape[1], mlp_w.shape[0]
    return (
        ranks == LINE * CORES
        and towers in (1, 2, 4)
        and pooled.shape[0] == 2
        and E % height == 0
        and height % 16 == 0
        and hid % 128 == 0
        and (pooled.shape[2] // ranks) % 128 == 0
    )


def solution(mesh):
    def on_device(*args):
        if fits(mesh, args[0], args[6]):
            return in_one_kernel(mesh.shape["tower"], mesh.shape["rank"], *args)
        return by_collectives(*args)

    return jax.shard_map(
        on_device,
        mesh=mesh,
        in_specs=(
            P(None, ("tower", "rank"), None),
            P("tower", None),
            P("tower", None, None, None),
            P("tower", None, None),
            P("tower", None, None),
            P("tower", None),
            P(("tower", "rank"), None),
            P(("tower", "rank")),
            P(("tower", "rank")),
        ),
        out_specs=P(None, "rank", "tower"),
        check_vma=False,
    )
```

```python
import functools

import jax
import jax.numpy as jnp
from jax import lax
from jax.experimental import pallas as pl
from jax.experimental.pallas import tpu as pltpu
from jax.sharding import PartitionSpec as P

E = 128
CD = 128
CORES = 2
LINE = 4

epsilon = 1e-06
MESH = pl.DeviceIdType.MESH


def drain(ref, sem):
    pltpu.make_async_copy(ref, ref, sem).wait()


def fused(
    n_tower,
    n_rank,
    order_any,
    pooled,
    cross_w,
    cross_b,
    compress,
    gain,
    mlp_w,
    hid_b,
    hid_o,
    out,
    order,
    arrived,
    weights,
    compress_v,
    bias_v,
    flat_v,
    gain_v,
    bias_c,
    gain_c,
    first,
    state_a,
    state_b,
    towers,
    mixed,
    rows,
    packs,
    flat,
    hid_c,
    score,
    parts,
    aside,
    known,
    load_sem,
    sent,
    a2a_recv,
    row_recv,
    pack_recv,
    tower_recv,
    mix_recv,
    part_recv,
):
    micro = pooled.shape[0]
    block = arrived[0].shape[-1]
    layers, td = cross_w.shape[1], cross_w.shape[2]
    hid = mlp_w.shape[0]
    chunks = [(b, j) for b in range(micro) for j in range(CORES)]
    t = lax.axis_index("tower")
    r = lax.axis_index("rank")
    z = r // CORES
    c = lax.rem(r, CORES)
    mate = z * CORES + (1 - c)
    half = z // 2
    here, there = 1 + half, 2 - half
    near, far = 3 * half, 3 * (1 - half)
    inner = z == here
    outer = z != here
    steps = [1 << i for i in range(n_tower.bit_length() - 1)]

    barrier = pltpu.get_barrier_semaphore()

    def greet(**device):
        pl.semaphore_signal(barrier, inc=1, device_id=device, device_id_type=MESH)

    own_loads = [
        pltpu.make_async_copy(
            pooled.at[b, :, pl.ds(pl.multiple_of(((2 * half + c) * CORES + j) * block, block), block)],
            arrived[q].at[r],
            a2a_recv.at[q],
        )
        for q, (b, j) in enumerate(chunks)
    ]
    own_packs = [pltpu.make_async_copy(ref, packs.at[half, z % 2, i], pack_recv.at[0]) for i, ref in enumerate((hid_b, hid_o))]
    loads = [
        pltpu.make_async_copy(cross_b, bias_v, load_sem.at[0]),
        pltpu.make_async_copy(gain, gain_v, load_sem.at[0]),
        pltpu.make_async_copy(compress.at[0], compress_v, load_sem.at[0]),
        pltpu.make_async_copy(mlp_w, rows.at[half, pl.ds((z % 2) * hid, hid)], load_sem.at[0]),
        pltpu.make_async_copy(order_any, order, load_sem.at[0]),
    ]
    w_loads = [pltpu.make_async_copy(cross_w.at[0, l], weights.at[l], load_sem.at[1]) for l in range(layers)]

    def send_block(q, chip, core):
        b, j = chunks[q]
        rank = ((chip // 2) * 2 + core) * CORES + j
        pltpu.make_async_remote_copy(
            src_ref=pooled.at[b, :, pl.ds(pl.multiple_of(rank * block, block), block)],
            dst_ref=arrived[q].at[r],
            send_sem=sent.at[0],
            recv_sem=a2a_recv.at[q],
            device_id={"rank": chip * CORES + core},
            device_id_type=MESH,
        ).start()

    def send_rows(chip, group):
        pltpu.make_async_remote_copy(
            src_ref=mlp_w,
            dst_ref=rows.at[half, pl.ds((z % 2) * hid, hid)],
            send_sem=sent.at[0],
            recv_sem=row_recv.at[group],
            device_id={"rank": chip * CORES + c},
            device_id_type=MESH,
        ).start()

    def send_packs(chip):
        for i, ref in enumerate((hid_b, hid_o)):
            pltpu.make_async_remote_copy(
                src_ref=ref,
                dst_ref=packs.at[half, z % 2, i],
                send_sem=sent.at[0],
                recv_sem=pack_recv.at[0],
                device_id={"rank": chip * CORES + c},
                device_id_type=MESH,
            ).start()

    @pl.when(outer)
    def _():
        pl.semaphore_wait(barrier, 2 * CORES)
        for chip in (there, here):
            send_packs(chip)
        for q in range(len(chunks)):
            for chip in (there, here):
                for core in (c, 1 - c):
                    send_block(q, chip, core)
        send_rows(here, 0)
        send_rows(there, 2)

    width = block // n_tower

    def finish(count):
        drain(parts.at[:count], part_recv.at[0])
        logits = parts[0]
        for u in range(1, n_tower * CORES):
            logits = logits + parts[u]
        for u in range(n_tower):

            @pl.when(t == u)
            def _():
                for b in range(micro):
                    out[b] = logits[:, b * block + u * width : b * block + (u + 1) * width]

    @pl.when(inner)
    def _():
        for chip in (far, there, near):
            for k in range(CORES):
                greet(rank=chip * CORES + k)
        greet(rank=mate)
        for d in steps:
            greet(tower=t ^ d)
        for copy in own_loads + own_packs + loads + w_loads:
            copy.start()
        pl.semaphore_wait(barrier, 2 * CORES - 1 + len(steps))
        if len(steps) > 1:
            pl.semaphore_signal(known.at[0], inc=1, device_id={"tower": t ^ 1}, device_id_type=MESH)
        send_packs(there)
        for q in range(len(chunks)):
            for core in (c, 1 - c):
                send_block(q, there, core)
            send_block(q, here, 1 - c)
        send_rows(there, 1)

        for copy in loads:
            copy.wait()
        for l in range(layers):
            flat_v[l : l + 1, :] = bias_v[l]
        bias_c[...] = flat_v[...].T
        gain_c[...] = jnp.broadcast_to(gain_v[...], (8, CD)).T
        for q in range(len(chunks)):
            score[q] = jnp.zeros(score.shape[1:], jnp.float32)

        per_feature = n_rank // order.shape[1]
        height = arrived[0].shape[1]

        def tower(q):
            cols = slice(q * block, (q + 1) * block)
            drain(arrived[q], a2a_recv.at[q])
            for slot in range(order.shape[1]):
                feature = order[0, slot]
                for h in range(per_feature):
                    first[slot * E + h * height : slot * E + (h + 1) * height, cols] = arrived[q][
                        feature * per_feature + h
                    ]

            current, spare = first, state_a
            for l in range(layers):
                if q == 0 and l == 0:
                    for copy in w_loads:
                        copy.wait()
                for m in range(0, td, E):
                    at = slice(m, m + E)
                    product = (
                        jnp.dot(weights[l, at, :], current[:, cols], preferred_element_type=jnp.float32)
                        + bias_c[at, l : l + 1]
                    )
                    spare[at, cols] = (
                        first[at, cols].astype(jnp.float32) * product
                        + current[at, cols].astype(jnp.float32)
                    ).astype(jnp.bfloat16)
                current, spare = spare, (state_b if spare is state_a else state_a)
            squeezed = jnp.dot(compress_v[...], current[:, cols], preferred_element_type=jnp.float32)
            inverse_rms = lax.rsqrt(jnp.mean(squeezed * squeezed, axis=0, keepdims=True) + epsilon)
            towers[q][t] = (squeezed * inverse_rms * gain_c[:, 0:1]).astype(jnp.bfloat16)
            if q == 0 and len(steps) > 1:
                pl.semaphore_wait(known.at[0], 1)
            for d in range(n_tower - 1, 0, -1):
                pltpu.make_async_remote_copy(
                    src_ref=towers[q].at[t],
                    dst_ref=towers[q].at[t],
                    send_sem=sent.at[0],
                    recv_sem=tower_recv.at[q],
                    device_id={"tower": t ^ d},
                    device_id_type=MESH,
                ).start()

        def mix(q):
            drain(towers[q].at[: n_tower - 1], tower_recv.at[q])
            values = [towers[q][u].astype(jnp.float32) for u in range(n_tower)]
            gram = {}
            for u in range(n_tower):
                for v in range(u, n_tower):
                    gram[u, v] = gram[v, u] = jnp.sum(values[u] * values[v], axis=0, keepdims=True) / CD
            for u in range(n_tower):
                total = values[u]
                for v in range(n_tower):
                    total = total + gram[u, v] * values[v]
                mixed[q][u * CD : (u + 1) * CD, :block] = total.astype(jnp.bfloat16)
                if u % 2:
                    part = pl.ds((u - 1) * CD, 2 * CD)
                    pltpu.make_async_remote_copy(
                        src_ref=mixed[q].at[part, pl.ds(0, block)],
                        dst_ref=mixed[q].at[part, pl.ds(block, block)],
                        send_sem=sent.at[0],
                        recv_sem=mix_recv.at[q],
                        device_id={"rank": mate},
                        device_id_type=MESH,
                    ).start()

        def mate_mixed(q):
            drain(mixed[q].at[:, pl.ds(block, block)], mix_recv.at[q])

        def add(q, pair, sides=range(CORES)):
            cols = slice(sides[0] * block, (sides[-1] + 1) * block)
            hidden = jnp.dot(rows[pair], mixed[q][:, cols], preferred_element_type=jnp.float32)
            bias, weight = hid_c[pair, 0], hid_c[pair, 1]
            for i, k in enumerate(sides):
                at = slice(k * block, (k + 1) * block)
                terms = jnp.maximum(hidden[:, i * block : (i + 1) * block] + bias, 0.0) * weight
                score[q, :, at] = score[q, :, at] + jnp.sum(terms.reshape(-1, 8, block), axis=0)

        def add_one(q, chip):
            here_rows = pl.ds(pl.multiple_of((chip % 2) * hid, hid), hid)
            hidden = jnp.dot(rows[1 - half, here_rows, :], mixed[q][...], preferred_element_type=jnp.float32)
            bias, weight = hid_c[1 - half, 0, here_rows, :], hid_c[1 - half, 1, here_rows, :]
            for k in range(CORES):
                at = slice(k * block, (k + 1) * block)
                terms = jnp.maximum(hidden[:, at] + bias, 0.0) * weight
                score[q, :, at] = score[q, :, at] + jnp.sum(terms.reshape(-1, 8, block), axis=0)

        def prepare():
            drain(packs, pack_recv.at[0])
            for s in range(LINE):
                for i in range(2):
                    flat[2 * s + i : 2 * s + i + 1, :] = packs[s // 2, s % 2, i].astype(jnp.float32)
            turned = flat[...].T
            for s in range(LINE):
                for i in range(2):
                    hid_c[s // 2, i, (s % 2) * hid : (s % 2 + 1) * hid, :] = jnp.broadcast_to(
                        turned[:, 2 * s + i : 2 * s + i + 1], (hid, block)
                    )

        me = t * CORES + c

        def settle(side, j):
            k = c if side == 0 else 1 - c
            rank = (2 * half + k) * CORES + j
            for b in range(micro):
                at = slice(b * block, (b + 1) * block)
                cols = slice(side * block, (side + 1) * block)
                aside[k, j, :, at] = jnp.sum(score[b * CORES + j, :, cols], axis=0, keepdims=True)

            def hand_over(d):
                pltpu.make_async_remote_copy(
                    src_ref=aside.at[k, j],
                    dst_ref=parts.at[me],
                    send_sem=sent.at[0],
                    recv_sem=part_recv.at[0],
                    device_id={"tower": t ^ d, "rank": rank},
                    device_id_type=MESH,
                ).start()

            for d in range(n_tower - 1, 0, -1):
                hand_over(d)
            pl.when(rank != r)(functools.partial(hand_over, 0))

        count = len(chunks)
        prepare()
        for q in range(count):
            tower(q)
        mix(0)
        mix(1)
        mix(2)
        drain(rows.at[0, pl.ds(0, hid)], row_recv.at[0])
        for q in range(2):
            mate_mixed(q)
            add(q, half)
        mate_mixed(2)
        add(2, half)
        drain(rows.at[0, pl.ds(0, hid)], row_recv.at[1])
        for q in range(3):
            add_one(q, there)
        mix(3)
        add(3, half, [0])
        drain(rows.at[0, pl.ds(0, hid)], row_recv.at[2])
        add_one(0, far)
        add_one(2, far)
        settle(1, 0)
        settle(0, 0)
        add_one(1, far)
        add(3, 1 - half, [0])
        settle(0, 1)
        mate_mixed(3)
        add(3, half, [1])
        add(3, 1 - half, [1])
        settle(1, 1)

        parts[me] = aside[1 - half, c]

        for q in range(count):
            drain(arrived[q].at[:CORES + 1], sent.at[0])
            drain(towers[q].at[: n_tower - 1], sent.at[0])
            drain(mixed[q].at[:, pl.ds(0, block)], sent.at[0])
        drain(packs.at[0, 0], sent.at[0])
        drain(rows.at[0, pl.ds(0, hid)], sent.at[0])
        finish(n_tower * CORES - 1)
        drain(parts, sent.at[0])
        drain(parts.at[: n_tower * CORES - 1], sent.at[0])

    @pl.when(outer)
    def _():
        for q in range(len(chunks)):
            drain(arrived[q].at[: 2 * CORES], sent.at[0])
        drain(packs.at[0], sent.at[0])
        drain(rows.at[0], sent.at[0])
        finish(n_tower * CORES)


def in_one_kernel(
    n_tower, n_rank, pooled, order, cross_w, cross_b, compress, gain, mlp_w, mlp_bias, out_weight
):
    micro, height, samples = pooled.shape
    block = samples // n_rank
    _, layers, td, _ = cross_w.shape
    hid, width = mlp_w.shape
    chips = n_rank // CORES
    count = micro * CORES
    every = count * block
    bf16, f32 = jnp.bfloat16, jnp.float32
    dma = pltpu.SemaphoreType.DMA
    hbm = pl.BlockSpec(memory_space=pl.ANY)
    return pl.pallas_call(
        functools.partial(fused, n_tower, n_rank),
        out_shape=pltpu.VMEM((micro, 1, block // n_tower), f32),
        in_specs=[hbm] * 9,
        out_specs=pl.BlockSpec(memory_space=pltpu.VMEM),
        scratch_shapes=[
            pltpu.SMEM(order.shape, order.dtype),
            [pltpu.VMEM((n_rank, height, block), bf16)] * count,
            pltpu.VMEM((layers, td, td), bf16),
            pltpu.VMEM((CD, td), bf16),
            pltpu.VMEM((layers, 1, td), f32),
            pltpu.VMEM((8, td), f32),
            pltpu.VMEM((1, CD), f32),
            pltpu.VMEM((td, 8), f32),
            pltpu.VMEM((CD, 8), f32),
            pltpu.VMEM((td, every), bf16),
            pltpu.VMEM((td, every), bf16),
            pltpu.VMEM((td, every), bf16),
            [pltpu.VMEM((n_tower, CD, block), bf16)] * count,
            [pltpu.VMEM((width, CORES * block), bf16)] * count,
            pltpu.VMEM((2, 2 * hid, width), bf16),
            pltpu.VMEM((2, 2, 2, 1, hid), bf16),
            pltpu.VMEM((2 * chips, hid), f32),
            pltpu.VMEM((2, 2, 2 * hid, block), f32),
            pltpu.VMEM((count, 8, CORES * block), f32),
            pltpu.VMEM((n_tower * CORES, 1, micro * block), f32),
            pltpu.VMEM((CORES, CORES, 1, micro * block), f32),
            pltpu.SemaphoreType.REGULAR((1,)),
            dma((2,)),
            dma((1,)),
            dma((count,)),
            dma((3,)),
            dma((1,)),
            dma((count,)),
            dma((count,)),
            dma((1,)),
        ],
        compiler_params=pltpu.CompilerParams(collective_id=0, has_side_effects=True),
    )(
        order,
        pooled,
        cross_w,
        cross_b.swapaxes(0, 1),
        compress,
        gain,
        mlp_w,
        mlp_bias[None],
        out_weight[None],
    )


def tower_block(first, weights, biases, compress, gain):
    first_f = first.astype(jnp.float32)
    current = first
    for layer in range(weights.shape[0]):
        product = (
            jnp.dot(weights[layer], current, preferred_element_type=jnp.float32)
            + biases[layer][:, None]
        )
        current = (first_f * product + current.astype(jnp.float32)).astype(jnp.bfloat16)
    squeezed = jnp.dot(compress, current, preferred_element_type=jnp.float32)
    inverse_rms = lax.rsqrt(jnp.mean(squeezed * squeezed, axis=0, keepdims=True) + epsilon)
    return (squeezed * inverse_rms * gain[:, None]).astype(jnp.bfloat16)


def interact(joined):
    samples_now = joined.shape[1]
    values_f = joined.astype(jnp.float32).reshape(-1, CD, samples_now)
    gram = jnp.einsum("tck,uck->tuk", values_f, values_f, precision=lax.Precision.HIGHEST) / CD
    mixed = values_f + jnp.einsum("tuk,uck->tck", gram, values_f, precision=lax.Precision.HIGHEST)
    return mixed.reshape(-1, samples_now).astype(jnp.bfloat16)


def logit_terms(hidden_rows, hidden_bias, hidden_out, features):
    hidden = (
        jnp.dot(hidden_rows, features, preferred_element_type=jnp.float32)
        + hidden_bias.astype(jnp.float32)[:, None]
    )
    return jnp.sum(
        jax.nn.relu(hidden) * hidden_out.astype(jnp.float32)[:, None], axis=0, keepdims=True
    )


def by_collectives(
    pooled,
    feature_order,
    cross_weight,
    cross_bias,
    compress_weight,
    norm_gain,
    mlp_weight,
    mlp_bias,
    out_weight,
):
    micro_count = pooled.shape[0]
    arriving = [
        lax.all_to_all(pooled[batch], "rank", split_axis=1, concat_axis=0, tiled=True)
        for batch in range(micro_count)
    ]
    hidden_rows, hidden_bias, hidden_out = (
        lax.all_gather(mlp_weight, "rank", axis=0, tiled=True),
        lax.all_gather(mlp_bias, "rank", axis=0, tiled=True),
        lax.all_gather(out_weight, "rank", axis=0, tiled=True),
    )
    results = []
    for batch in range(micro_count):
        arrived = arriving[batch]
        samples_here = arrived.shape[1]
        first = jnp.take(arrived.reshape(-1, E, samples_here), feature_order[0], axis=0).reshape(
            -1, samples_here
        )
        compressed = tower_block(
            first, cross_weight[0], cross_bias[0], compress_weight[0], norm_gain[0]
        )
        all_towers = lax.all_gather(compressed, "tower", axis=0, tiled=True)
        partial_value = logit_terms(hidden_rows, hidden_bias, hidden_out, interact(all_towers))
        logit_row = lax.psum_scatter(partial_value, "tower", scatter_dimension=1, tiled=True)
        results.append(logit_row)
    return jnp.stack(results)


def fits(mesh, pooled, mlp_w):
    towers, ranks = mesh.shape["tower"], mesh.shape["rank"]
    height, hid = pooled.shape[1], mlp_w.shape[0]
    return (
        ranks == LINE * CORES
        and towers in (1, 2, 4)
        and pooled.shape[0] == 2
        and E % height == 0
        and height % 16 == 0
        and hid % 128 == 0
        and (pooled.shape[2] // ranks) % 128 == 0
    )


def solution(mesh):
    def on_device(*args):
        if fits(mesh, args[0], args[6]):
            return in_one_kernel(mesh.shape["tower"], mesh.shape["rank"], *args)
        return by_collectives(*args)

    return jax.shard_map(
        on_device,
        mesh=mesh,
        in_specs=(
            P(None, ("tower", "rank"), None),
            P("tower", None),
            P("tower", None, None, None),
            P("tower", None, None),
            P("tower", None, None),
            P("tower", None),
            P(("tower", "rank"), None),
            P(("tower", "rank")),
            P(("tower", "rank")),
        ),
        out_specs=P(None, "rank", "tower"),
        check_vma=False,
    )
```
